128 devices in a mesh: tm: 8 (over y, core), asset: 16 (over x, z).
Axes of the slice: x: 4, y: 4, z: 4, core: 2. Of those that a mesh axis runs over, the one named last changes fastest.
Arguments:
- features: bfloat16 [16, 20480, 512], P('tm', 'asset'), may hold values from -6 to 6
- w_value: bfloat16 [512, 512], replicated, may hold values from -0.25 to 0.25
- w_gate: bfloat16 [512, 512], replicated, may hold values from -0.25 to 0.25
- cotangent: bfloat16 [16, 20480, 512], P('tm', 'asset'), may hold values from -6 to 6
- local_rows: int32 [320], P('asset'), may hold values from 0 to 9
- local_cols: int32 [320], P('asset'), may hold values from 0 to 9
- local_count: int32 [16], P('asset'), may hold values from 10 to 20, as said below
- local_tiles: bfloat16 [320, 128, 128], P('asset'), may hold values from -0.3125 to 0.3125
- remote_rows: int32 [256], P('asset'), may hold values from 0 to 9
- remote_cols: int32 [256], P('asset'), may hold values from 0 to 9
- remote_live: int32 [256], P('asset'), may hold values from 0 to 1, as said below
- remote_tiles: bfloat16 [256, 128, 128], P('asset'), may hold values from -0.3125 to 0.3125
Outputs:
- output: bfloat16 [16, 20480, 512], P('tm', 'asset')
- grad_features: bfloat16 [16, 20480, 512], P('tm', 'asset')
- grad_value: float32 [512, 512], replicated
- grad_gate: float32 [512, 512], replicated
The draws below stay inside these ranges and needn't reach their ends.
Inputs may be any that keep to these rules, and one draw needn't show every extreme that they name: `local_count`: used local slots of each index of asset; some index uses all 20 in every draw. `remote_live`: at most one remote tile for each pair of indices of asset, never from an index to itself; in every draw some index holds a tile for every other index, and some index receives a tile from every other index.
All inputs are finite; a program needn't handle non-finite values.
Results may differ from the reference program's by a relative error of at most 0.0057.
Values may be sent and summed in bfloat16 or wider, within the bound.
A program may use at most 128 MiB of HBM per device.

```python
import jax
import jax.numpy as jnp
from jax import lax

D = 512
TILE = 128
BLK_DEV = 10
LOC = 20
ASSETS = 20480
TIME = 16
N_ASSET = 16


def draw_local_count(key, part):
    key_base = jax.random.fold_in(key, 11)
    first, second = jax.random.split(key_base)
    counts = jax.random.randint(first, (N_ASSET,), BLK_DEV, LOC + 1)
    chosen = jax.random.randint(second, (), 0, N_ASSET)
    return jnp.where(jnp.arange(N_ASSET) == chosen, LOC, counts).astype(jnp.int32)


def draw_remote_live(key, part):
    key_base = jax.random.fold_in(key, 23)
    first, second, third = jax.random.split(key_base, 3)
    live = (jax.random.randint(first, (N_ASSET, N_ASSET), 0, 5) < 3).astype(jnp.int32)
    sender = jax.random.randint(second, (), 0, N_ASSET)
    receiver = jax.random.randint(third, (), 0, N_ASSET)
    source = jnp.arange(N_ASSET)[:, None]
    target = jnp.arange(N_ASSET)[None, :]
    live = jnp.where(source == sender, 1, live)
    live = jnp.where(target == receiver, 1, live)
    live = jnp.where(source == target, 0, live)
    return live.reshape(-1).astype(jnp.int32)


def touch_ends(result, own_key, least, high):
    index_at = [jax.random.randint(jax.random.fold_in(own_key, axis), (), 0, length) for axis, length in enumerate(result.shape)]
    widest = result.shape.index(max(result.shape))
    beside = index_at[:widest] + [(index_at[widest] + 1) % result.shape[widest]] + index_at[widest + 1:]
    return result.at[tuple(index_at)].set(least).at[tuple(beside)].set(high)


def block_levels(stream_key, dims, pieces, low, top_value):
    loudness, own = 1.0, jax.random.fold_in(stream_key, 6)
    for dim, parts in pieces:
        draws = jnp.exp(jax.random.uniform(jax.random.fold_in(own, dim), (parts,), jnp.float32, low / len(pieces), top_value / len(pieces)))
        loudness = loudness * jnp.repeat(draws, dims[dim] // parts).reshape([-1 if axis == dim else 1 for axis in range(len(dims))])
    return loudness


def noise(key, extent, scale, limit, shards=(), kind=jnp.bfloat16):
    level = block_levels(key, extent, shards, -0.22, 0.18) if shards else 1.0
    result = jax.random.normal(key, extent, jnp.float32) * scale * level
    return jnp.minimum(jnp.maximum(result, -limit), limit).astype(kind)


def setup_inputs(seed: int = 0) -> dict:
    splits = jax.random.split(jax.random.key(seed), 13)
    features = noise(splits[0], (TIME, ASSETS, D), 1.0, 6.0, ((0, 8), (1, 16)))
    w_value = noise(splits[1], (D, D), D ** -0.5, 0.25)
    w_gate = noise(splits[2], (D, D), D ** -0.5, 0.25)
    cotangent = noise(splits[3], (TIME, ASSETS, D), 1.0, 6.0, ((0, 8), (1, 16)))
    local_rows = touch_ends(jax.random.randint(splits[4], (N_ASSET * LOC,), 0, BLK_DEV), jax.random.fold_in(splits[4], 1), 0, BLK_DEV - 1).astype(jnp.int32)
    local_cols = touch_ends(jax.random.randint(splits[5], (N_ASSET * LOC,), 0, BLK_DEV), jax.random.fold_in(splits[5], 1), 0, BLK_DEV - 1).astype(jnp.int32)
    local_count = draw_local_count(jax.random.fold_in(splits[12], 71), 0)
    local_tiles = noise(splits[7], (N_ASSET * LOC, TILE, TILE), (3 * TILE) ** -0.5, 0.3125, ((0, 16),))
    remote_rows = touch_ends(jax.random.randint(splits[8], (N_ASSET * N_ASSET,), 0, BLK_DEV), jax.random.fold_in(splits[8], 1), 0, BLK_DEV - 1).astype(jnp.int32)
    remote_cols = touch_ends(jax.random.randint(splits[9], (N_ASSET * N_ASSET,), 0, BLK_DEV), jax.random.fold_in(splits[9], 1), 0, BLK_DEV - 1).astype(jnp.int32)
    remote_live = draw_remote_live(jax.random.fold_in(splits[12], 71), 0)
    remote_tiles = noise(splits[11], (N_ASSET * N_ASSET, TILE, TILE), (3 * TILE) ** -0.5, 0.3125, ((0, 16),))
    return dict(features=features, w_value=w_value, w_gate=w_gate, cotangent=cotangent, local_rows=local_rows, local_cols=local_cols, local_count=local_count, local_tiles=local_tiles, remote_rows=remote_rows, remote_cols=remote_cols, remote_live=remote_live, remote_tiles=remote_tiles)


def tile_lists(local_rows, local_cols, local_count, local_tiles, remote_rows, remote_cols, remote_live, remote_tiles):
    slot = jnp.arange(N_ASSET * LOC, dtype=jnp.int32)
    owner = slot // LOC
    lrow = owner * BLK_DEV + local_rows
    lcol = owner * BLK_DEV + local_cols
    lmask = (slot % LOC < local_count[owner]).astype(jnp.float32)
    entry = jnp.arange(N_ASSET * N_ASSET, dtype=jnp.int32)
    source = entry // N_ASSET
    target = entry % N_ASSET
    rrow = target * BLK_DEV + remote_rows[target * N_ASSET + source]
    rcol = source * BLK_DEV + remote_cols
    rmask = remote_live.astype(jnp.float32)
    rows = jnp.concatenate([lrow, rrow]).astype(jnp.int32)
    cols = jnp.concatenate([lcol, rcol]).astype(jnp.int32)
    masks = jnp.concatenate([lmask, rmask])
    tiles = jnp.concatenate([local_tiles, remote_tiles], axis=0)
    return rows, cols, masks, tiles


def reference(features, w_value, w_gate, cotangent, local_rows, local_cols, local_count, local_tiles, remote_rows, remote_cols, remote_live, remote_tiles):
    blocks_all = N_ASSET * BLK_DEV
    flat = features.reshape(-1, D)
    value = jnp.dot(flat, w_value, preferred_element_type=jnp.float32).astype(jnp.bfloat16)
    gate = jax.nn.sigmoid(jnp.dot(flat, w_gate, preferred_element_type=jnp.float32))
    value_blocks = value.reshape(TIME, blocks_all, TILE, D)
    rows, cols, masks, tiles = tile_lists(local_rows, local_cols, local_count, local_tiles, remote_rows, remote_cols, remote_live, remote_tiles)

    def forward_step(total, item):
        row, col, mask, tile = item
        block = lax.dynamic_index_in_dim(value_blocks, col, 1, keepdims=False)
        term = jnp.einsum("ij,tjd->tid", tile.astype(jnp.float32), block.astype(jnp.float32)).astype(jnp.bfloat16)
        old = lax.dynamic_index_in_dim(total, row, 1, keepdims=False)
        new = old + term.astype(jnp.float32) * mask
        return lax.dynamic_update_index_in_dim(total, new, row, 1), None

    start = jnp.zeros((TIME, blocks_all, TILE, D), jnp.float32)
    agg_blocks, _ = lax.scan(forward_step, start, (rows, cols, masks, tiles))
    agg = agg_blocks.reshape(-1, D)
    output = (flat.astype(jnp.float32) + gate * agg).astype(jnp.bfloat16)
    grad_out = cotangent.reshape(-1, D).astype(jnp.float32)
    dagg = (grad_out * gate).astype(jnp.bfloat16)
    dgate = (grad_out * agg * gate * (1.0 - gate)).astype(jnp.bfloat16)
    dagg_blocks = dagg.reshape(TIME, blocks_all, TILE, D)

    def backward_step(total, item):
        row, col, mask, tile = item
        block = lax.dynamic_index_in_dim(dagg_blocks, row, 1, keepdims=False)
        term = jnp.einsum("ji,tjd->tid", tile.astype(jnp.float32), block.astype(jnp.float32)).astype(jnp.bfloat16)
        old = lax.dynamic_index_in_dim(total, col, 1, keepdims=False)
        new = old + term.astype(jnp.float32) * mask
        return lax.dynamic_update_index_in_dim(total, new, col, 1), None

    dvalue_blocks, _ = lax.scan(backward_step, start, (rows, cols, masks, tiles))
    dvalue = dvalue_blocks.reshape(-1, D).astype(jnp.bfloat16)
    grad_features = grad_out + jnp.dot(dvalue, w_value.T, preferred_element_type=jnp.float32)
    grad_features = grad_features + jnp.dot(dgate, w_gate.T, preferred_element_type=jnp.float32)
    scale = (TIME * ASSETS) ** -0.5
    grad_value = jnp.dot(flat.T, dvalue, preferred_element_type=jnp.float32) * scale
    grad_gate = jnp.dot(flat.T, dgate, preferred_element_type=jnp.float32) * scale
    return (output.reshape(TIME, ASSETS, D), grad_features.astype(jnp.bfloat16).reshape(TIME, ASSETS, D), grad_value, grad_gate)
```

```python
import functools

import jax
import jax.numpy as jnp
from jax import lax
from jax.experimental import pallas as pl
from jax.experimental.pallas import tpu as pltpu
from jax.sharding import PartitionSpec as P

MESH = pl.DeviceIdType.MESH
F32 = jnp.float32
BF16 = jnp.bfloat16
NX, NZ, NY, NC = 4, 4, 4, 2
STEPS, BLOCKS, TILE, D = 2, 10, 128, 512
PEERS = NX * NZ - 1
LOC = 20
ZERO = BLOCKS + LOC
ROWS = STEPS * BLOCKS
SCALE = float(16 * 20480) ** -0.5


def offset(k):
    j = k - 3
    pair = j // 2
    odd = j % 2
    near_dx = 1 + 2 * odd
    near_dz = jnp.where(odd == 0, pair, (4 - pair) % 4)
    far_dz = j - 8
    dx = jnp.where(k < 3, 0, jnp.where(k < 11, near_dx, 2))
    dz = jnp.where(k < 3, k + 1, jnp.where(k < 11, near_dz, far_dz))
    return dx, dz


def place():
    asset, tm = lax.axis_index("asset"), lax.axis_index("tm")
    return asset // NZ, asset % NZ, tm // NC, tm % NC


def sent_to(k):
    x, z, _, _ = place()
    dx, dz = offset(k)
    return (x + dx) % NX * NZ + (z + dz) % NZ


def came_from(k):
    x, z, _, _ = place()
    dx, dz = offset(k)
    return (x + NX - dx) % NX * NZ + (z + NZ - dz) % NZ


def chain_tables(rows, cols, count, rrows, rcols, links, heads):
    live = count[0]

    def local_link(src, way):
        def entry(l, _):
            mine = src[l]
            found = jnp.int32(ZERO)
            for m in range(LOC):
                hit = (src[m] == mine) & (m < l) & (m < live)
                found = jnp.where(hit, BLOCKS + m, found)
            links[way, l] = found
            return 0

        lax.fori_loop(0, LOC, entry, 0)

        def head(r, _):
            found = jnp.int32(ZERO)
            for m in range(LOC):
                found = jnp.where((src[m] == r) & (m < live), BLOCKS + m, found)
            heads[way, r] = found
            return 0

        lax.fori_loop(0, BLOCKS, head, 0)

    def remote_link(src, way):
        def entry(k, _):
            mine = src[came_from(k)]
            found = mine
            for m in range(PEERS):
                hit = (src[came_from(m)] == mine) & (m < k)
                found = jnp.where(hit, BLOCKS + m, found)
            links[way, k] = found
            return 0

        lax.fori_loop(0, PEERS, entry, 0)

        def head(r, _):
            found = r
            for m in range(PEERS):
                found = jnp.where(src[came_from(m)] == r, BLOCKS + m, found)
            heads[way, r] = found
            return 0

        lax.fori_loop(0, BLOCKS, head, 0)

    local_link(rows, 0)
    remote_link(rrows, 1)
    local_link(cols, 2)
    remote_link(rcols, 3)


def dot(a, b, ca, cb):
    return lax.dot_general(a, b, (((ca,), (cb,)), ((), ())), preferred_element_type=F32)


def kernel(
    rows, cols, count, rrows, rcols, rlive,
    feat_hbm, cot_hbm, wv_hbm, wg_hbm, lt_hbm, rt_hbm,
    out_hbm, gf_hbm, gv_hbm, gg_hbm,
    feat, cot, wv, wg, lt, rt,
    sf, rf, sb, rb, slots, gate, dagg, gsum, dgate, outs,
    part, core_in, acc, y_in, mine, xz_in, full,
    links, heads,
    load_sem, store_sem, sf_sem, rf_sem, sb_sem, rb_sem,
    core_s, core_r, y_s, y_r, xz_s, xz_r,
):
    x, z, y, c = place()
    asset, tm = lax.axis_index("asset"), lax.axis_index("tm")

    loads = []
    for i, (src, dst) in enumerate(
        ((feat_hbm, feat), (rt_hbm, rt), (wg_hbm, wg), (cot_hbm, cot), (lt_hbm, lt), (wv_hbm, wv))
    ):
        copy = pltpu.make_async_copy(src, dst, load_sem.at[i])
        copy.start()
        loads.append(copy)

    def core_peer():
        return (y * NC + (1 - c), asset)

    def y_peer(dy):
        return ((y + dy) % NY * NC + c, asset)

    barrier = pltpu.get_barrier_semaphore()

    def greet(k, _):
        pl.semaphore_signal(barrier, inc=1, device_id=(tm, sent_to(k)), device_id_type=MESH)
        return 0

    lax.fori_loop(0, PEERS, greet, 0)
    for dy in (1, 2, 3):
        pl.semaphore_signal(barrier, inc=1, device_id=y_peer(dy), device_id_type=MESH)
    pl.semaphore_signal(barrier, inc=1, device_id=core_peer(), device_id_type=MESH)
    pl.semaphore_wait(barrier, PEERS + 4)

    def exchange(k, src, dst, ssem, rsem):
        return pltpu.make_async_remote_copy(
            src_ref=src.at[k], dst_ref=dst.at[k], send_sem=ssem.at[k], recv_sem=rsem.at[k],
            device_id=(tm, sent_to(k)), device_id_type=MESH,
        )

    def masked(peer):
        return (rt[peer].astype(F32) * rlive[peer].astype(F32)).astype(BF16)

    loads[0].wait()
    loads[1].wait()

    def send_term(k, _):
        peer = sent_to(k)
        tile = masked(peer)
        col = rcols[peer]
        for t in range(STEPS):
            sf[k, t] = dot(tile, feat[t * BLOCKS + col], 1, 0).astype(BF16)
        exchange(k, sf, rf, sf_sem, rf_sem).start()
        return 0

    lax.fori_loop(0, PEERS, send_term, 0)

    loads[2].wait()
    loads[3].wait()

    def gate_step(i, _):
        logits = dot(feat[pl.ds(2 * i, 2)].reshape(2 * TILE, D), wg[...], 1, 0)
        g = jax.nn.sigmoid(logits).reshape(2, TILE, D)
        gate[pl.ds(2 * i, 2)] = g
        dagg[pl.ds(2 * i, 2)] = (cot[pl.ds(2 * i, 2)].astype(F32) * g).astype(BF16)
        return 0

    lax.fori_loop(0, ROWS // 2, gate_step, 0)

    def send_back(k, _):
        row = rrows[sent_to(k)]
        for t in range(STEPS):
            sb[k, t] = dagg[t * BLOCKS + row]
        exchange(k, sb, rb, sb_sem, rb_sem).start()
        return 0

    lax.fori_loop(0, PEERS, send_back, 0)

    chain_tables(rows, cols, count, rrows, rcols, links, heads)
    slots[ZERO] = jnp.zeros((STEPS, TILE, D), F32)
    loads[4].wait()

    def local_chain(src, blocks, way, side):
        def entry(l, _):
            tile = lt[l]
            other = src[l]
            for t in range(STEPS):
                slots[BLOCKS + l, t] = slots[links[way, l], t] + dot(tile, blocks[t * BLOCKS + other], side, 0)
            return 0

        lax.fori_loop(0, LOC, entry, 0)

        def base(r, _):
            slots[r] = slots[heads[way, r]]
            return 0

        lax.fori_loop(0, BLOCKS, base, 0)

    local_chain(cols, feat, 0, 1)

    def take_term(k, _):
        exchange(k, sf, rf, sf_sem, rf_sem).wait_recv()
        slots[BLOCKS + k] = slots[links[1, k]] + rf[k].astype(F32)
        return 0

    lax.fori_loop(0, PEERS, take_term, 0)
    loads[5].wait()

    def middle(i, _):
        t, r = i // (BLOCKS // 2), i % (BLOCKS // 2) * 2
        at = pl.ds(2 * i, 2)
        gsum[2 * i] = slots[heads[1, r], t].astype(BF16)
        gsum[2 * i + 1] = slots[heads[1, r + 1], t].astype(BF16)
        agg = dot(gsum[at].reshape(2 * TILE, D), wv[...], 1, 0).reshape(2, TILE, D)
        g = gate[at]
        outs[at] = (feat[at].astype(F32) + g * agg).astype(BF16)
        dgate[at] = (cot[at].astype(F32) * agg * g * (1.0 - g)).astype(BF16)
        return 0

    lax.fori_loop(0, ROWS // 2, middle, 0)
    out_copy = pltpu.make_async_copy(outs, out_hbm, store_sem.at[0])
    out_copy.start()

    part[...] = jnp.zeros_like(part)

    def weight_step(i, _):
        at = pl.ds(4 * i, 4)
        part[0] += dot(gsum[at].reshape(4 * TILE, D), dagg[at].reshape(4 * TILE, D), 0, 0)
        part[1] += dot(feat[at].reshape(4 * TILE, D), dgate[at].reshape(4 * TILE, D), 0, 0)
        return 0

    lax.fori_loop(0, ROWS // 4, weight_step, 0)

    core_copy = pltpu.make_async_remote_copy(
        src_ref=part.at[1 - c], dst_ref=core_in, send_sem=core_s.at[0], recv_sem=core_r.at[0],
        device_id=core_peer(), device_id_type=MESH,
    )
    core_copy.start()

    def pre_step(i, _):
        at = pl.ds(2 * i, 2)
        gate[at] = cot[at].astype(F32) + dot(dgate[at].reshape(2 * TILE, D), wg[...], 1, 1).reshape(2, TILE, D)
        return 0

    lax.fori_loop(0, ROWS // 2, pre_step, 0)

    core_copy.wait_recv()
    acc[...] = part[c] + core_in[...]

    def y_copy(dy):
        return pltpu.make_async_remote_copy(
            src_ref=acc.at[pl.ds((y + dy) % NY * TILE, TILE)], dst_ref=y_in.at[dy - 1],
            send_sem=y_s.at[dy - 1], recv_sem=y_r.at[dy - 1], device_id=y_peer(dy), device_id_type=MESH,
        )

    y_copies = [y_copy(dy) for dy in (1, 3, 2)]
    for copy in y_copies:
        copy.start()

    local_chain(rows, dagg, 2, 0)

    for copy in y_copies:
        copy.wait_recv()
    mine[...] = acc[pl.ds(y * TILE, TILE), :] + y_in[0] + y_in[1] + y_in[2]

    def spread(k):
        return pltpu.make_async_remote_copy(
            src_ref=mine.at[pl.ds(sent_to(k) * 8, 8)], dst_ref=xz_in.at[k],
            send_sem=xz_s.at[k], recv_sem=xz_r.at[k], device_id=(tm, sent_to(k)), device_id_type=MESH,
        )

    def gather(k):
        return pltpu.make_async_remote_copy(
            src_ref=full.at[c, y, asset], dst_ref=full.at[c, y, asset],
            send_sem=xz_s.at[PEERS + k], recv_sem=xz_r.at[PEERS + k], device_id=(tm, sent_to(k)), device_id_type=MESH,
        )

    def each(count, do):
        def step(k, _):
            do(k)
            return 0

        lax.fori_loop(0, count, step, 0)

    def take_back(k):
        exchange(k, sb, rb, sb_sem, rb_sem).wait_recv()
        tile = masked(came_from(k))
        for t in range(STEPS):
            slots[BLOCKS + k, t] = slots[links[3, k], t] + dot(tile, rb[k, t], 0, 0)

    each(PEERS, lambda k: spread(k).start())
    each(8, take_back)
    each(PEERS, lambda k: spread(k).wait_recv())
    total = mine[pl.ds(asset * 8, 8), :]
    for k in range(PEERS):
        total = total + xz_in[k]
    full[c, y, asset] = total * SCALE
    each(PEERS, lambda k: gather(k).start())
    each(PEERS - 8, lambda k: take_back(k + 8))
    each(PEERS, lambda k: gather(k).wait_recv())

    def y_gather(dy):
        return pltpu.make_async_remote_copy(
            src_ref=full.at[c, y], dst_ref=full.at[c, y], send_sem=y_s.at[2 + dy], recv_sem=y_r.at[2 + dy],
            device_id=y_peer(dy), device_id_type=MESH,
        )

    y_gathers = [y_gather(dy) for dy in (1, 3, 2)]
    for copy in y_gathers:
        copy.start()
    out_copy.wait()

    def finish(i, _):
        t, r = i // (BLOCKS // 2), i % (BLOCKS // 2) * 2
        at = pl.ds(2 * i, 2)
        gsum[2 * i] = slots[heads[3, r], t].astype(BF16)
        gsum[2 * i + 1] = slots[heads[3, r + 1], t].astype(BF16)
        grad = gate[at] + dot(gsum[at].reshape(2 * TILE, D), wv[...], 1, 1).reshape(2, TILE, D)
        outs[at] = grad.astype(BF16)
        return 0

    lax.fori_loop(0, ROWS // 2, finish, 0)
    grad_copy = pltpu.make_async_copy(outs, gf_hbm, store_sem.at[1])
    grad_copy.start()

    for copy in y_gathers:
        copy.wait_recv()
    core_gather = pltpu.make_async_remote_copy(
        src_ref=full.at[c], dst_ref=full.at[c], send_sem=core_s.at[1], recv_sem=core_r.at[1],
        device_id=core_peer(), device_id_type=MESH,
    )
    core_gather.start()
    core_gather.wait_recv()
    gv_copy = pltpu.make_async_copy(full.at[0], gv_hbm, store_sem.at[2])
    gg_copy = pltpu.make_async_copy(full.at[1], gg_hbm, store_sem.at[3])
    gv_copy.start()
    gg_copy.start()

    def sent(k):
        exchange(k, sf, rf, sf_sem, rf_sem).wait_send()
        exchange(k, sb, rb, sb_sem, rb_sem).wait_send()
        spread(k).wait_send()
        gather(k).wait_send()

    each(PEERS, sent)
    core_copy.wait_send()
    core_gather.wait_send()
    for copy in y_copies + y_gathers:
        copy.wait_send()
    grad_copy.wait()
    gv_copy.wait()
    gg_copy.wait()


def per_device(
    features, w_value, w_gate, cotangent, local_rows, local_cols, local_count, local_tiles,
    remote_rows, remote_cols, remote_live, remote_tiles,
):
    smem = pl.BlockSpec(memory_space=pltpu.SMEM)
    hbm = pl.BlockSpec(memory_space=pl.ANY)
    dma = pltpu.SemaphoreType.DMA
    blocks = (ROWS, TILE, D)
    exchanged = (PEERS, STEPS, TILE, D)
    out, grad, gv, gg = pl.pallas_call(
        kernel,
        name="relation",
        out_shape=(
            jax.ShapeDtypeStruct(blocks, BF16),
            jax.ShapeDtypeStruct(blocks, BF16),
            jax.ShapeDtypeStruct((NY, NX * NZ, 8, D), F32),
            jax.ShapeDtypeStruct((NY, NX * NZ, 8, D), F32),
        ),
        in_specs=[smem] * 6 + [hbm] * 6,
        out_specs=(hbm,) * 4,
        scratch_shapes=[
            pltpu.VMEM(blocks, BF16),
            pltpu.VMEM(blocks, BF16),
            pltpu.VMEM((D, D), BF16),
            pltpu.VMEM((D, D), BF16),
            pltpu.VMEM((LOC, TILE, TILE), BF16),
            pltpu.VMEM((NX * NZ, TILE, TILE), BF16),
            pltpu.VMEM(exchanged, BF16),
            pltpu.VMEM(exchanged, BF16),
            pltpu.VMEM(exchanged, BF16),
            pltpu.VMEM(exchanged, BF16),
            pltpu.VMEM((ZERO + 1, STEPS, TILE, D), F32),
            pltpu.VMEM(blocks, F32),
            pltpu.VMEM(blocks, BF16),
            pltpu.VMEM(blocks, BF16),
            pltpu.VMEM(blocks, BF16),
            pltpu.VMEM(blocks, BF16),
            pltpu.VMEM((2, D, D), F32),
            pltpu.VMEM((D, D), F32),
            pltpu.VMEM((D, D), F32),
            pltpu.VMEM((NY - 1, TILE, D), F32),
            pltpu.VMEM((TILE, D), F32),
            pltpu.VMEM((PEERS, 8, D), F32),
            pltpu.VMEM((2, NY, NX * NZ, 8, D), F32),
            pltpu.SMEM((4, LOC), jnp.int32),
            pltpu.SMEM((4, BLOCKS), jnp.int32),
            dma((6,)),
            dma((4,)),
            dma((PEERS,)),
            dma((PEERS,)),
            dma((PEERS,)),
            dma((PEERS,)),
            dma((2,)),
            dma((2,)),
            dma((6,)),
            dma((6,)),
            dma((2 * PEERS,)),
            dma((2 * PEERS,)),
        ],
        compiler_params=pltpu.CompilerParams(
            collective_id=0, has_side_effects=True, vmem_limit_bytes=67043328
        ),
    )(
        local_rows, local_cols, local_count, remote_rows, remote_cols, remote_live,
        features.reshape(blocks), cotangent.reshape(blocks), w_value, w_gate, local_tiles, remote_tiles,
    )
    return (
        out.reshape(features.shape),
        grad.reshape(features.shape),
        gv.reshape(D, D),
        gg.reshape(D, D),
    )


def solution(mesh):
    return jax.shard_map(
        per_device,
        mesh=mesh,
        in_specs=(
            P("tm", "asset", None),
            P(),
            P(),
            P("tm", "asset", None),
            P("asset"),
            P("asset"),
            P("asset"),
            P("asset", None, None),
            P("asset"),
            P("asset"),
            P("asset"),
            P("asset", None, None),
        ),
        out_specs=(P("tm", "asset", None), P("tm", "asset", None), P(), P()),
        check_vma=False,
    )
```

```python
import functools

import jax
import jax.numpy as jnp
from jax import lax
from jax.experimental import pallas as pl
from jax.experimental.pallas import tpu as pltpu
from jax.sharding import PartitionSpec as P

MESH = pl.DeviceIdType.MESH
F32 = jnp.float32
BF16 = jnp.bfloat16
NX, NZ, NY, NC = 4, 4, 4, 2
STEPS, BLOCKS, TILE, D = 2, 10, 128, 512
PEERS = NX * NZ - 1
LOC = 20
ZERO = BLOCKS + LOC
ROWS = STEPS * BLOCKS
WIDE = 5
SCALE = float(16 * 20480) ** -0.5


HOPS = (1, 3, 2)
ORDER = [(s, 0) for s in HOPS] + [(0, j) for j in HOPS] + [(s, j) for s in HOPS for j in HOPS]


def pick(i, values):
    found = values[-1]
    for n, value in enumerate(values[:-1]):
        found = jnp.where(i == n, value, found)
    return found


def place():
    asset, tm = lax.axis_index("asset"), lax.axis_index("tm")
    return asset // NZ, asset % NZ, tm // NC, tm % NC


def at_distance(dx, dz):
    x, z, _, _ = place()
    return (x + dx) % NX * NZ + (z + dz) % NZ


def from_distance(dx, dz):
    return at_distance(NX - dx, NZ - dz)


def turned(h, first, second):
    return jnp.where(h == 0, first, second), jnp.where(h == 0, second, first)


def chain_tables(rows, cols, count, rrows, rcols, links, heads):
    live = count[0]

    def table(keys, way, start):
        for n, key in enumerate(keys):
            found = start(key)
            for m in range(n):
                found = jnp.where(keys[m] == key, BLOCKS + m, found)
            links[way, n] = found
        for r in range(BLOCKS):
            found = start(r)
            for m, key in enumerate(keys):
                found = jnp.where(key == r, BLOCKS + m, found)
            heads[way, r] = found

    for way, src in ((0, rows), (1, cols)):
        table([jnp.where(n < live, src[n], -1) for n in range(LOC)], way, lambda key: ZERO)
    for h in range(STEPS):
        for way, src in ((2, rrows), (4, rcols)):
            table([src[from_distance(*((s, j), (j, s))[h])] for s, j in ORDER], way + h, lambda key: key)


def dot(a, b, ca, cb):
    return lax.dot_general(a, b, (((ca,), (cb,)), ((), ())), preferred_element_type=F32)


def each(first, last, do):
    def step(k, _):
        do(k)
        return 0

    lax.fori_loop(first, last, step, 0)


def kernel(
    rows, cols, count, rrows, rcols, rlive,
    feat_hbm, cot_hbm, wv_hbm, wg_hbm, lt_hbm, rt_hbm,
    outs, gsum, full,
    feat, cot, wv, wg, lt, rt,
    away, over, last, slots, gate, dagg, dgate,
    part, core_in, acc, y_in, mine, xz_in,
    links, heads,
    load_sem, ex_s, ex_r,
    core_s, core_r, y_s, y_r, xz_s, xz_r,
):
    x, z, y, c = place()
    asset, tm = lax.axis_index("asset"), lax.axis_index("tm")

    loads = []
    for i, (src, dst) in enumerate(
        ((feat_hbm, feat), (rt_hbm, rt), (wg_hbm, wg), (cot_hbm, cot), (lt_hbm, lt), (wv_hbm, wv))
    ):
        copy = pltpu.make_async_copy(src, dst, load_sem.at[i])
        copy.start()
        loads.append(copy)

    def core_peer():
        return (y * NC + (1 - c), asset)

    def y_peer(dy):
        return ((y + dy) % NY * NC + c, asset)

    def other(k):
        return (asset + 1 + k) % (NX * NZ)

    barrier = pltpu.get_barrier_semaphore()
    each(0, PEERS, lambda k: pl.semaphore_signal(barrier, inc=1, device_id=(tm, other(k)), device_id_type=MESH))
    for dy in (1, 2, 3):
        pl.semaphore_signal(barrier, inc=1, device_id=y_peer(dy), device_id_type=MESH)
    pl.semaphore_signal(barrier, inc=1, device_id=core_peer(), device_id_type=MESH)

    def first_hop(e, h, d):
        return pltpu.make_async_remote_copy(
            src_ref=away.at[h, d - 1], dst_ref=over.at[e, h, d],
            send_sem=ex_s.at[e, h, d, 0], recv_sem=ex_r.at[e, h, d, 0],
            device_id=(tm, at_distance(*turned(h, d, 0))), device_id_type=MESH,
        )

    def second_hop(e, h, s, j):
        return pltpu.make_async_remote_copy(
            src_ref=over.at[e, h, s, j], dst_ref=last.at[e, h, s, j - 1],
            send_sem=ex_s.at[e, h, s, j], recv_sem=ex_r.at[e, h, s, j],
            device_id=(tm, at_distance(*turned(h, 0, j))), device_id_type=MESH,
        )

    def masked(peer):
        return (rt[peer].astype(F32) * rlive[peer].astype(F32)).astype(BF16)

    def send(e, block, ready):
        def fill(i):
            d, h = pick(i // 2, HOPS), i % 2
            for j in range(4):
                away[h, d - 1, j] = block(h, at_distance(*turned(h, d, j)))

        def go(i):
            first_hop(e, i % 2, pick(i // 2, HOPS)).start()

        def both(i):
            fill(i)
            go(i)

        each(0, 2, fill)
        ready()
        each(0, 2, go)
        each(2, 6, both)

        def own(h):
            for j in (1, 2, 3):
                over[e, h, 0, j] = block(h, at_distance(*turned(h, 0, j)))

        each(0, 2, own)

        def hand(i):
            second_hop(e, i % 2, 0, pick(i // 2, HOPS)).start()

        each(0, 6, hand)

    def relay(e, first, end):
        def step(i):
            s, h = pick(i // 2, HOPS), i % 2
            first_hop(e, h, s).wait_recv()
            for j in (1, 3, 2):
                second_hop(e, h, s, j).start()

        each(first, end, step)

    loads[0].wait()
    loads[1].wait()

    def term(h, peer):
        return dot(masked(peer), feat[h * BLOCKS + rcols[peer]], 1, 0).astype(BF16)

    send(0, term, lambda: pl.semaphore_wait(barrier, PEERS + 4))

    loads[2].wait()
    loads[3].wait()

    def gate_step(i):
        at = pl.ds(WIDE * i, WIDE)
        logits = dot(feat[at].reshape(WIDE * TILE, D), wg[...], 1, 0)
        g = jax.nn.sigmoid(logits).reshape(WIDE, TILE, D)
        gate[at] = g
        dagg[at] = (cot[at].astype(F32) * g).astype(BF16)

    each(0, ROWS // WIDE, gate_step)
    chain_tables(rows, cols, count, rrows, rcols, links, heads)
    slots[ZERO] = jnp.zeros((STEPS, TILE, D), F32)
    loads[4].wait()

    def local_chain(src, blocks, way, side):
        def entry(l):
            tile = lt[l]
            other_block = src[l]
            for t in range(STEPS):
                slots[BLOCKS + l, t] = slots[links[way, l], t] + dot(tile, blocks[t * BLOCKS + other_block], side, 0)

        each(0, LOC, entry)

        def base(r):
            slots[r] = slots[heads[way, r]]

        each(0, BLOCKS, base)

    local_chain(cols, feat, 0, 1)
    relay(0, 0, 6)

    def sent_away(e):
        each(0, 6, lambda i: first_hop(e, i % 2, i // 2 + 1).wait_send())

    sent_away(0)

    def owed(h, peer):
        return dagg[h * BLOCKS + rrows[peer]]

    send(1, owed, lambda: None)

    def take_near(e, add):
        def direct(i):
            s, h = pick(i // 2, HOPS), i % 2
            add(i // 2, h, from_distance(*turned(h, s, 0)), over[e, h, s, 0])

        def handed(i):
            j, h = pick(i // 2, HOPS), i % 2
            second_hop(e, h, 0, j).wait_recv()
            add(3 + i // 2, h, from_distance(*turned(h, 0, j)), last[e, h, 0, j - 1])

        each(0, 6, direct)
        each(0, 6, handed)

    def take_far(e, add):
        def across(i):
            k, h = i // 2, i % 2
            s, j = pick(k // 3, HOPS), pick(k % 3, HOPS)
            second_hop(e, h, s, j).wait_recv()
            add(6 + k, h, from_distance(*turned(h, s, j)), last[e, h, s, j - 1])

        each(0, 18, across)

    def add_term(k, h, peer, block):
        slots[BLOCKS + k, h] = slots[links[2 + h, k], h] + block.astype(F32)

    take_near(0, add_term)
    take_far(0, add_term)
    loads[5].wait()

    def summed(way, i):
        t, r = WIDE * i // BLOCKS, WIDE * i % BLOCKS
        return jnp.concatenate([slots[heads[way + t, r + n], t].astype(BF16) for n in range(WIDE)])

    def middle(i):
        at = pl.ds(WIDE * i, WIDE)
        total = summed(2, i)
        gsum[at] = total.reshape(WIDE, TILE, D)
        agg = dot(total, wv[...], 1, 0).reshape(WIDE, TILE, D)
        g = gate[at]
        outs[at] = (feat[at].astype(F32) + g * agg).astype(BF16)
        dgate[at] = (cot[at].astype(F32) * agg * g * (1.0 - g)).astype(BF16)

    each(0, ROWS // WIDE, middle)
    part[...] = jnp.zeros_like(part)

    def weight_step(i, _):
        at = pl.ds(4 * i, 4)
        part[0] += dot(gsum[at].reshape(4 * TILE, D), dagg[at].reshape(4 * TILE, D), 0, 0)
        part[1] += dot(feat[at].reshape(4 * TILE, D), dgate[at].reshape(4 * TILE, D), 0, 0)
        return 0

    lax.fori_loop(0, ROWS // 4, weight_step, 0)

    core_copy = pltpu.make_async_remote_copy(
        src_ref=part.at[1 - c], dst_ref=core_in, send_sem=core_s.at[0], recv_sem=core_r.at[0],
        device_id=core_peer(), device_id_type=MESH,
    )
    core_copy.start()
    core_copy.wait_recv()
    acc[...] = (part[c] + core_in[...]).astype(BF16)

    def y_copy(dy):
        return pltpu.make_async_remote_copy(
            src_ref=acc.at[pl.ds((y + dy) % NY * TILE, TILE)], dst_ref=y_in.at[dy - 1],
            send_sem=y_s.at[dy - 1], recv_sem=y_r.at[dy - 1], device_id=y_peer(dy), device_id_type=MESH,
        )

    y_copies = [y_copy(dy) for dy in (1, 3, 2)]
    for copy in y_copies:
        copy.start()

    local_chain(rows, dagg, 1, 0)
    own_rows = pl.ds(y * TILE, TILE)
    mine[...] = part[c, own_rows, :] + core_in[own_rows, :]

    for copy in y_copies:
        copy.wait_recv()
    mine[...] += y_in[0].astype(F32) + y_in[1].astype(F32) + y_in[2].astype(F32)

    def spread(k):
        return pltpu.make_async_remote_copy(
            src_ref=mine.at[pl.ds(other(k) * 8, 8)], dst_ref=xz_in.at[k],
            send_sem=xz_s.at[k], recv_sem=xz_r.at[k], device_id=(tm, other(k)), device_id_type=MESH,
        )

    def gather(k):
        return pltpu.make_async_remote_copy(
            src_ref=full.at[c, y, asset], dst_ref=full.at[c, y, asset],
            send_sem=xz_s.at[PEERS + k], recv_sem=xz_r.at[PEERS + k], device_id=(tm, other(k)), device_id_type=MESH,
        )

    each(0, PEERS, lambda k: spread(k).start())
    relay(1, 0, 4)

    def pre_step(i):
        at = pl.ds(WIDE * i, WIDE)
        gate[at] = cot[at].astype(F32) + dot(dgate[at].reshape(WIDE * TILE, D), wg[...], 1, 1).reshape(WIDE, TILE, D)

    each(0, ROWS // WIDE, pre_step)

    each(0, PEERS, lambda k: spread(k).wait_recv())
    total = mine[pl.ds(asset * 8, 8), :]
    for k in range(PEERS):
        total = total + xz_in[k]
    full[c, y, asset] = (total * SCALE).astype(BF16)
    each(0, PEERS, lambda k: gather(k).start())

    def add_back(k, h, peer, block):
        slots[BLOCKS + k, h] = slots[links[4 + h, k], h] + dot(masked(peer), block, 0, 0)

    relay(1, 4, 6)
    take_near(1, add_back)
    each(0, PEERS, lambda k: gather(k).wait_recv())

    def y_gather(dy):
        return pltpu.make_async_remote_copy(
            src_ref=full.at[c, y], dst_ref=full.at[c, y], send_sem=y_s.at[2 + dy], recv_sem=y_r.at[2 + dy],
            device_id=y_peer(dy), device_id_type=MESH,
        )

    y_gathers = [y_gather(dy) for dy in (1, 3, 2)]
    for copy in y_gathers:
        copy.start()
    take_far(1, add_back)
    for copy in y_gathers:
        copy.wait_recv()
    core_gather = pltpu.make_async_remote_copy(
        src_ref=full.at[c], dst_ref=full.at[c], send_sem=core_s.at[1], recv_sem=core_r.at[1],
        device_id=core_peer(), device_id_type=MESH,
    )
    core_gather.start()

    def finish(i):
        at = pl.ds(WIDE * i, WIDE)
        gsum[at] = (gate[at] + dot(summed(4, i), wv[...], 1, 1).reshape(WIDE, TILE, D)).astype(BF16)

    each(0, ROWS // WIDE, finish)
    core_gather.wait_recv()
    sent_away(1)

    def handed(i):
        for e in range(2):
            for j in (1, 2, 3):
                second_hop(e, i % 2, i // 2, j).wait_send()

    each(0, 8, handed)

    def sent(k):
        spread(k).wait_send()
        gather(k).wait_send()

    each(0, PEERS, sent)
    core_copy.wait_send()
    core_gather.wait_send()
    for copy in y_copies + y_gathers:
        copy.wait_send()


def emit(outs, gsum, full, out_hbm, gf_hbm, gv_hbm, gg_hbm, wide, sem):
    copies = [pltpu.make_async_copy(outs, out_hbm, sem.at[0]), pltpu.make_async_copy(gsum, gf_hbm, sem.at[1])]
    for copy in copies:
        copy.start()
    for i, dst in enumerate((gv_hbm, gg_hbm)):
        wide[i] = full[i].astype(F32)
        copies.append(pltpu.make_async_copy(wide.at[i], dst, sem.at[2 + i]))
        copies[-1].start()
    for copy in copies:
        copy.wait()


def per_device(
    features, w_value, w_gate, cotangent, local_rows, local_cols, local_count, local_tiles,
    remote_rows, remote_cols, remote_live, remote_tiles,
):
    smem = pl.BlockSpec(memory_space=pltpu.SMEM)
    hbm = pl.BlockSpec(memory_space=pl.ANY)
    vmem = pl.BlockSpec(memory_space=pltpu.VMEM)
    dma = pltpu.SemaphoreType.DMA
    blocks = (ROWS, TILE, D)
    reduced = (2, NY, NX * NZ, 8, D)
    held = pl.pallas_call(
        kernel,
        name="relation",
        out_shape=(pltpu.VMEM(blocks, BF16), pltpu.VMEM(blocks, BF16), pltpu.VMEM(reduced, BF16)),
        in_specs=[smem] * 6 + [hbm] * 6,
        out_specs=(vmem,) * 3,
        scratch_shapes=[
            pltpu.VMEM(blocks, BF16),
            pltpu.VMEM(blocks, BF16),
            pltpu.VMEM((D, D), BF16),
            pltpu.VMEM((D, D), BF16),
            pltpu.VMEM((LOC, TILE, TILE), BF16),
            pltpu.VMEM((NX * NZ, TILE, TILE), BF16),
            pltpu.VMEM((2, 3, 4, TILE, D), BF16),
            pltpu.VMEM((2, 2, 4, 4, TILE, D), BF16),
            pltpu.VMEM((2, 2, 4, 3, TILE, D), BF16),
            pltpu.VMEM((ZERO + 1, STEPS, TILE, D), F32),
            pltpu.VMEM(blocks, F32),
            pltpu.VMEM(blocks, BF16),
            pltpu.VMEM(blocks, BF16),
            pltpu.VMEM((2, D, D), F32),
            pltpu.VMEM((D, D), F32),
            pltpu.VMEM((D, D), BF16),
            pltpu.VMEM((NY - 1, TILE, D), BF16),
            pltpu.VMEM((TILE, D), F32),
            pltpu.VMEM((PEERS, 8, D), F32),
            pltpu.SMEM((6, LOC), jnp.int32),
            pltpu.SMEM((6, BLOCKS), jnp.int32),
            dma((6,)),
            dma((2, 2, 4, 4)),
            dma((2, 2, 4, 4)),
            dma((2,)),
            dma((2,)),
            dma((6,)),
            dma((6,)),
            dma((2 * PEERS,)),
            dma((2 * PEERS,)),
        ],
        compiler_params=pltpu.CompilerParams(
            collective_id=0, has_side_effects=True, vmem_limit_bytes=57 << 20
        ),
    )(
        local_rows, local_cols, local_count, remote_rows, remote_cols, remote_live,
        features.reshape(blocks), cotangent.reshape(blocks), w_value, w_gate, local_tiles, remote_tiles,
    )
    wide = jax.ShapeDtypeStruct(reduced[1:], F32)
    out, grad, gv, gg = pl.pallas_call(
        emit,
        name="emit",
        out_shape=(jax.ShapeDtypeStruct(blocks, BF16), jax.ShapeDtypeStruct(blocks, BF16), wide, wide),
        in_specs=[vmem] * 3,
        out_specs=(hbm,) * 4,
        scratch_shapes=[pltpu.VMEM(reduced, F32), dma((4,))],
        compiler_params=pltpu.CompilerParams(vmem_limit_bytes=16 << 20),
    )(*[pltpu.with_memory_space_constraint(a, pltpu.MemorySpace.VMEM) for a in held])
    return (
        out.reshape(features.shape),
        grad.reshape(features.shape),
        gv.reshape(D, D),
        gg.reshape(D, D),
    )


def solution(mesh):
    return jax.shard_map(
        per_device,
        mesh=mesh,
        in_specs=(
            P("tm", "asset", None),
            P(),
            P(),
            P("tm", "asset", None),
            P("asset"),
            P("asset"),
            P("asset"),
            P("asset", None, None),
            P("asset"),
            P("asset"),
            P("asset"),
            P("asset", None, None),
        ),
        out_specs=(P("tm", "asset", None), P("tm", "asset", None), P(), P()),
        check_vma=False,
    )
```

```python
import functools

import jax
import jax.numpy as jnp
from jax import lax
from jax.experimental import pallas as pl
from jax.experimental.pallas import tpu as pltpu
from jax.sharding import PartitionSpec as P

MESH = pl.DeviceIdType.MESH
F32 = jnp.float32
BF16 = jnp.bfloat16
NX, NZ, NY, NC = 4, 4, 4, 2
STEPS, BLOCKS, TILE, D = 2, 10, 128, 512
PEERS = NX * NZ - 1
LOC = 20
ZERO = BLOCKS + LOC
ROWS = STEPS * BLOCKS
WIDE = 5
GROUP = 5
SCALE = float(16 * 20480) ** -0.5


HOPS = (1, 3, 2)
ORDER = [(s, 0) for s in HOPS] + [(0, j) for j in HOPS] + [(s, j) for s in HOPS for j in HOPS]


def pick(i, values):
    found = values[-1]
    for n, value in enumerate(values[:-1]):
        found = jnp.where(i == n, value, found)
    return found


def place():
    asset, tm = lax.axis_index("asset"), lax.axis_index("tm")
    return asset // NZ, asset % NZ, tm // NC, tm % NC


def at_distance(dx, dz):
    x, z, _, _ = place()
    return (x + dx) % NX * NZ + (z + dz) % NZ


def from_distance(dx, dz):
    return at_distance(NX - dx, NZ - dz)


def turned(h, first, second):
    return jnp.where(h == 0, first, second), jnp.where(h == 0, second, first)


def chain_tables(rows, cols, count, rrows, rcols, links, heads):
    live = count[0]

    def table(keys, way, start):
        for n, key in enumerate(keys):
            found = start(key)
            for m in range(n):
                found = jnp.where(keys[m] == key, BLOCKS + m, found)
            links[way, n] = found
        for r in range(BLOCKS):
            found = start(r)
            for m, key in enumerate(keys):
                found = jnp.where(key == r, BLOCKS + m, found)
            heads[way, r] = found

    for way, src in ((0, rows), (1, cols)):
        table([jnp.where(n < live, src[n], -1) for n in range(LOC)], way, lambda key: ZERO)
    for h in range(STEPS):
        for way, src in ((2, rrows), (4, rcols)):
            table([src[from_distance(*((s, j), (j, s))[h])] for s, j in ORDER], way + h, lambda key: key)


def dot(a, b, ca, cb):
    return lax.dot_general(a, b, (((ca,), (cb,)), ((), ())), preferred_element_type=F32)


def each(first, last, do):
    def step(k, _):
        do(k)
        return 0

    lax.fori_loop(first, last, step, 0)


def kernel(
    count, rows_hbm, cols_hbm, rrows_hbm, rcols_hbm, rlive_hbm,
    feat_hbm, cot_hbm, wv_hbm, wg_hbm, lt_hbm, rt_hbm,
    outs, gsum, gate, full, wv,
    rows, cols, rrows, rcols, rlive,
    feat, cot, wg, lt, rt,
    away, over, last, slots, dagg, dgate,
    part, core_in, acc, y_in, mine, mine_out, xz_in,
    links, heads,
    load_sem, ex_s, first_r, last_r,
    core_s, core_r, y_s, y_r, xz_s, xz_r,
):
    x, z, y, c = place()
    asset, tm = lax.axis_index("asset"), lax.axis_index("tm")

    loads = []
    for i, (src, dst) in enumerate(
        (
            (rcols_hbm, rcols),
            (rlive_hbm, rlive),
            (feat_hbm, feat),
            (rt_hbm, rt),
            (wg_hbm, wg),
            (cot_hbm, cot),
            (rows_hbm, rows),
            (cols_hbm, cols),
            (rrows_hbm, rrows),
            (lt_hbm, lt),
            (wv_hbm, wv),
        )
    ):
        copy = pltpu.make_async_copy(src, dst, load_sem.at[i])
        copy.start()
        loads.append(copy)

    def core_peer():
        return (y * NC + (1 - c), asset)

    def y_peer(dy):
        return ((y + dy) % NY * NC + c, asset)

    def other(k):
        return (asset + 1 + k) % (NX * NZ)

    barrier = pltpu.get_barrier_semaphore()
    each(0, PEERS, lambda k: pl.semaphore_signal(barrier, inc=1, device_id=(tm, other(k)), device_id_type=MESH))
    for dy in (1, 2, 3):
        pl.semaphore_signal(barrier, inc=1, device_id=y_peer(dy), device_id_type=MESH)
    pl.semaphore_signal(barrier, inc=1, device_id=core_peer(), device_id_type=MESH)

    def first_hop(e, h, d):
        return pltpu.make_async_remote_copy(
            src_ref=away.at[h, d - 1], dst_ref=over.at[e, h, d],
            send_sem=ex_s.at[e, 0], recv_sem=first_r.at[e, h, d - 1],
            device_id=(tm, at_distance(*turned(h, d, 0))), device_id_type=MESH,
        )

    def second_hop(e, h, s, j):
        return pltpu.make_async_remote_copy(
            src_ref=over.at[e, h, s, j], dst_ref=last.at[e, h, s, j - 1],
            send_sem=ex_s.at[e, 1], recv_sem=last_r.at[e, h, s],
            device_id=(tm, at_distance(*turned(h, 0, j))), device_id_type=MESH,
        )

    def masked(peer):
        return (rt[peer].astype(F32) * rlive[peer].astype(F32)).astype(BF16)

    def all_of(src, dst, ssem, rsem):
        return pltpu.make_async_remote_copy(
            src_ref=src, dst_ref=dst, send_sem=ssem, recv_sem=rsem, device_id=core_peer(), device_id_type=MESH
        )

    def arrived(e, h, s):
        all_of(last.at[e, h, s], last.at[e, h, s], ex_s.at[e, 1], last_r.at[e, h, s]).wait_recv()

    def send(e, block, ready):
        def fill(i):
            d, h = pick(i // 2, HOPS), i % 2
            for j in range(4):
                away[h, d - 1, j] = block(h, at_distance(*turned(h, d, j)))

        def go(i):
            first_hop(e, i % 2, pick(i // 2, HOPS)).start()

        def both(i):
            fill(i)
            go(i)

        fill(0)
        ready()
        go(0)
        each(1, 6, both)

        def own(h):
            for j in (1, 2, 3):
                over[e, h, 0, j] = block(h, at_distance(*turned(h, 0, j)))

        each(0, 2, own)

    def hand(e):
        def step(i):
            second_hop(e, i % 2, 0, pick(i // 2, HOPS)).start()

        each(0, 6, step)

    def relay(e, first, end):
        def step(i):
            s, h = pick(i // 2, HOPS), i % 2
            first_hop(e, h, s).wait_recv()
            for j in (1, 3, 2):
                second_hop(e, h, s, j).start()

        each(first, end, step)

    for copy in loads[:4]:
        copy.wait()

    def term(h, peer):
        return dot(masked(peer), feat[h * BLOCKS + rcols[peer]], 1, 0).astype(BF16)

    send(0, term, lambda: pl.semaphore_wait(barrier, PEERS + 4))
    hand(0)

    loads[4].wait()
    loads[5].wait()

    def gate_step(i):
        at = pl.ds(WIDE * i, WIDE)
        logits = dot(feat[at].reshape(WIDE * TILE, D), wg[...], 1, 0)
        g = jax.nn.sigmoid(logits).reshape(WIDE, TILE, D)
        gate[at] = g
        dagg[at] = (cot[at].astype(F32) * g).astype(BF16)

    each(0, ROWS // WIDE, gate_step)
    for copy in loads[6:10]:
        copy.wait()
    chain_tables(rows, cols, count, rrows, rcols, links, heads)
    slots[ZERO] = jnp.zeros((STEPS, TILE, D), F32)

    def local_chain(src, blocks, way, side):
        def entry(l):
            tile = lt[l]
            other_block = src[l]
            for t in range(STEPS):
                slots[BLOCKS + l, t] = slots[links[way, l], t] + dot(tile, blocks[t * BLOCKS + other_block], side, 0)

        each(0, LOC, entry)

        def base(r):
            slots[r] = slots[heads[way, r]]

        each(0, BLOCKS, base)

    local_chain(cols, feat, 0, 1)
    relay(0, 0, 6)

    def sent_away(e):
        all_of(away, away, ex_s.at[e, 0], first_r.at[e, 0, 0]).wait_send()

    sent_away(0)

    def owed(h, peer):
        return dagg[h * BLOCKS + rrows[peer]]

    send(1, owed, lambda: None)

    def take_near(e, add):
        def direct(i):
            s, h = pick(i // 2, HOPS), i % 2
            add(i // 2, h, from_distance(*turned(h, s, 0)), over[e, h, s, 0])

        def handed(i):
            j, h = pick(i // 2, HOPS), i % 2
            add(3 + i // 2, h, from_distance(*turned(h, 0, j)), last[e, h, 0, j - 1])

        each(0, 6, direct)
        each(0, 2, lambda h: arrived(e, h, 0))
        each(0, 6, handed)

    def take_far(e, first, end, add):
        def across(i):
            n, h = i // 2, i % 2
            s = pick(n, HOPS)
            arrived(e, h, s)
            for m, j in enumerate(HOPS):
                add(6 + 3 * n + m, h, from_distance(*turned(h, s, j)), last[e, h, s, j - 1])

        each(first, end, across)

    def add_term(k, h, peer, block):
        slots[BLOCKS + k, h] = slots[links[2 + h, k], h] + block.astype(F32)

    take_near(0, add_term)
    take_far(0, 0, 6, add_term)
    loads[10].wait()

    def summed(way, i):
        t, r = WIDE * i // BLOCKS, WIDE * i % BLOCKS
        return jnp.concatenate([slots[heads[way + t, r + n], t] for n in range(WIDE)])

    def middle(i):
        at = pl.ds(WIDE * i, WIDE)
        total = summed(2, i)
        high = total.astype(BF16)
        low = (total - high.astype(F32)).astype(BF16)
        gsum[at] = high.reshape(WIDE, TILE, D)
        agg = (dot(high, wv[...], 1, 0) + dot(low, wv[...], 1, 0)).reshape(WIDE, TILE, D)
        g = gate[at]
        outs[at] = (feat[at].astype(F32) + g * agg).astype(BF16)
        dgate[at] = (cot[at].astype(F32) * agg * g * (1.0 - g)).astype(BF16)

    each(0, ROWS // WIDE, middle)
    def weight(n, left, right):
        def product(i):
            at = pl.ds(BLOCKS * i, BLOCKS)
            return dot(left[at].reshape(BLOCKS * TILE, D), right[at].reshape(BLOCKS * TILE, D), 0, 0)

        part[n] = product(0)
        part[n] += product(1)

    core_copy = pltpu.make_async_remote_copy(
        src_ref=part.at[1 - c], dst_ref=core_in, send_sem=core_s.at[0], recv_sem=core_r.at[0],
        device_id=core_peer(), device_id_type=MESH,
    )
    weight(0, gsum, dagg)

    @pl.when(c == 1)
    def _():
        core_copy.start()

    weight(1, feat, dgate)

    @pl.when(c == 0)
    def _():
        core_copy.start()

    core_copy.wait_recv()
    acc[...] = (part[c] + core_in[...]).astype(BF16)

    def y_copy(dy):
        return pltpu.make_async_remote_copy(
            src_ref=acc.at[pl.ds((y + dy) % NY * TILE, TILE)], dst_ref=y_in.at[dy - 1],
            send_sem=y_s.at[0], recv_sem=y_r.at[0], device_id=y_peer(dy), device_id_type=MESH,
        )

    y_copies = [y_copy(dy) for dy in (1, 3, 2)]
    for copy in y_copies:
        copy.start()

    local_chain(rows, dagg, 1, 0)
    own_rows = pl.ds(y * TILE, TILE)
    mine[...] = part[c, own_rows, :] + core_in[own_rows, :]

    y_all = all_of(y_in, y_in, y_s.at[0], y_r.at[0])
    y_all.wait_recv()
    mine[...] += y_in[0].astype(F32) + y_in[1].astype(F32) + y_in[2].astype(F32)
    mine_out[...] = mine[...].reshape(NX * NZ, 8, D).astype(BF16)

    def spread(k):
        return pltpu.make_async_remote_copy(
            src_ref=mine_out.at[other(k)], dst_ref=xz_in.at[k],
            send_sem=xz_s.at[0], recv_sem=xz_r.at[0], device_id=(tm, other(k)), device_id_type=MESH,
        )

    def gather(k):
        return pltpu.make_async_remote_copy(
            src_ref=full.at[c, y, asset], dst_ref=full.at[c, y, asset],
            send_sem=xz_s.at[1], recv_sem=xz_r.at[1 + k // GROUP], device_id=(tm, other(k)), device_id_type=MESH,
        )

    each(0, PEERS, lambda k: spread(k).start())
    hand(1)
    relay(1, 0, 2)

    def pre_step(i):
        at = pl.ds(WIDE * i, WIDE)
        gate[at] = cot[at].astype(F32) + dot(dgate[at].reshape(WIDE * TILE, D), wg[...], 1, 1).reshape(WIDE, TILE, D)

    each(0, ROWS // WIDE, pre_step)

    spread_all = all_of(xz_in, xz_in, xz_s.at[0], xz_r.at[0])
    spread_all.wait_recv()
    total = mine[pl.ds(asset * 8, 8), :]
    for k in range(PEERS):
        total = total + xz_in[k].astype(F32)
    full[c, y, asset] = (total * SCALE).astype(BF16)
    each(0, PEERS, lambda k: gather(k).start())

    def add_back(k, h, peer, block):
        slots[BLOCKS + k, h] = slots[links[4 + h, k], h] + dot(masked(peer), block, 0, 0)

    relay(1, 2, 6)
    take_near(1, add_back)

    def hand_y(k, dy):
        piece = full.at[c, y, (asset + NX * NZ - 1 - k) % (NX * NZ)]
        return pltpu.make_async_remote_copy(
            src_ref=piece, dst_ref=piece, send_sem=y_s.at[1], recv_sem=y_r.at[1],
            device_id=y_peer(dy), device_id_type=MESH,
        )

    some = full.at[c, y, pl.ds(0, GROUP)]

    def pass_on(g):
        all_of(some, some, xz_s.at[1], xz_r.at[1 + g]).wait_recv()
        for k in range(GROUP):
            for dy in (1, 3, 2):
                hand_y(g * GROUP + k, dy).start()

    for dy in (1, 3, 2):
        hand_y(PEERS, dy).start()
    each(0, PEERS // GROUP, pass_on)
    take_far(1, 0, 4, add_back)
    most = full.at[c, pl.ds(0, NY - 1)]
    hand_all = all_of(most, most, y_s.at[1], y_r.at[1])
    hand_all.wait_recv()
    core_gather = pltpu.make_async_remote_copy(
        src_ref=full.at[c], dst_ref=full.at[c], send_sem=core_s.at[1], recv_sem=core_r.at[1],
        device_id=core_peer(), device_id_type=MESH,
    )
    core_gather.start()
    take_far(1, 4, 6, add_back)

    def settle(i):
        gsum[pl.ds(WIDE * i, WIDE)] = summed(4, i).astype(BF16).reshape(WIDE, TILE, D)

    each(0, ROWS // WIDE, settle)
    sent_away(1)
    for e in range(2):
        all_of(last.at[e], last.at[e], ex_s.at[e, 1], last_r.at[e, 0, 0]).wait_send()
    core_copy.wait_send()
    y_all.wait_send()
    spread_all.wait_send()
    pieces = full.at[c, y, pl.ds(0, PEERS)]
    all_of(pieces, pieces, xz_s.at[1], xz_r.at[1]).wait_send()
    hand_all.wait_send()
    core_gather.wait()


def emit(outs, dvalue, rest, full, wv, out_hbm, gf_hbm, gv_hbm, gg_hbm, grads, wide, sem):
    copies = [pltpu.make_async_copy(outs, out_hbm, sem.at[0])]
    copies[0].start()
    for i, dst in enumerate((gv_hbm, gg_hbm)):
        wide[i] = full[i].astype(F32)
        copies.append(pltpu.make_async_copy(wide.at[i], dst, sem.at[1 + i]))
        copies[-1].start()

    def chunk(i):
        at = pl.ds(WIDE * i, WIDE)
        return at, pltpu.make_async_copy(grads.at[at], gf_hbm.at[at], sem.at[3 + i])

    def finish(i):
        at, copy = chunk(i)
        back = dot(dvalue[at].reshape(WIDE * TILE, D), wv[...], 1, 1).reshape(WIDE, TILE, D)
        grads[at] = (rest[at] + back).astype(BF16)
        copy.start()

    each(0, ROWS // WIDE, finish)
    each(0, ROWS // WIDE, lambda i: chunk(i)[1].wait())
    for copy in copies:
        copy.wait()


def per_device(
    features, w_value, w_gate, cotangent, local_rows, local_cols, local_count, local_tiles,
    remote_rows, remote_cols, remote_live, remote_tiles,
):
    hbm = pl.BlockSpec(memory_space=pl.ANY)
    vmem = pl.BlockSpec(memory_space=pltpu.VMEM)
    dma = pltpu.SemaphoreType.DMA
    blocks = (ROWS, TILE, D)
    tables = (local_rows, local_cols, remote_rows, remote_cols, remote_live)
    reduced = (2, NY, NX * NZ, 8, D)
    held = pl.pallas_call(
        kernel,
        name="relation",
        out_shape=(
            pltpu.VMEM(blocks, BF16),
            pltpu.VMEM(blocks, BF16),
            pltpu.VMEM(blocks, F32),
            pltpu.VMEM(reduced, BF16),
            pltpu.VMEM((D, D), BF16),
        ),
        in_specs=[pl.BlockSpec(memory_space=pltpu.SMEM)] + [hbm] * 11,
        out_specs=(vmem,) * 5,
        scratch_shapes=[
            *(pltpu.SMEM(a.shape, jnp.int32) for a in tables),
            pltpu.VMEM(blocks, BF16),
            pltpu.VMEM(blocks, BF16),
            pltpu.VMEM((D, D), BF16),
            pltpu.VMEM((LOC, TILE, TILE), BF16),
            pltpu.VMEM((NX * NZ, TILE, TILE), BF16),
            pltpu.VMEM((2, 3, 4, TILE, D), BF16),
            pltpu.VMEM((2, 2, 4, 4, TILE, D), BF16),
            pltpu.VMEM((2, 2, 4, 3, TILE, D), BF16),
            pltpu.VMEM((ZERO + 1, STEPS, TILE, D), F32),
            pltpu.VMEM(blocks, BF16),
            pltpu.VMEM(blocks, BF16),
            pltpu.VMEM((2, D, D), F32),
            pltpu.VMEM((D, D), F32),
            pltpu.VMEM((D, D), BF16),
            pltpu.VMEM((NY - 1, TILE, D), BF16),
            pltpu.VMEM((TILE, D), F32),
            pltpu.VMEM((NX * NZ, 8, D), BF16),
            pltpu.VMEM((PEERS, 8, D), BF16),
            pltpu.SMEM((6, LOC), jnp.int32),
            pltpu.SMEM((6, BLOCKS), jnp.int32),
            dma((11,)),
            dma((2, 2)),
            dma((2, 2, 3)),
            dma((2, 2, 4)),
            dma((2,)),
            dma((2,)),
            dma((2,)),
            dma((2,)),
            dma((2,)),
            dma((1 + PEERS // GROUP,)),
        ],
        compiler_params=pltpu.CompilerParams(
            collective_id=0, has_side_effects=True, vmem_limit_bytes=54000000
        ),
    )(
        local_count, *tables,
        features.reshape(blocks), cotangent.reshape(blocks), w_value, w_gate, local_tiles, remote_tiles,
    )
    wide = jax.ShapeDtypeStruct(reduced[1:], F32)
    out, grad, gv, gg = pl.pallas_call(
        emit,
        name="emit",
        out_shape=(jax.ShapeDtypeStruct(blocks, BF16), jax.ShapeDtypeStruct(blocks, BF16), wide, wide),
        in_specs=[vmem] * 5,
        out_specs=(hbm,) * 4,
        scratch_shapes=[pltpu.VMEM(blocks, BF16), pltpu.VMEM(reduced, F32), dma((3 + ROWS // WIDE,))],
        compiler_params=pltpu.CompilerParams(vmem_limit_bytes=16 << 20),
    )(*[pltpu.with_memory_space_constraint(a, pltpu.MemorySpace.VMEM) for a in held])
    return (
        out.reshape(features.shape),
        grad.reshape(features.shape),
        gv.reshape(D, D),
        gg.reshape(D, D),
    )


def solution(mesh):
    return jax.shard_map(
        per_device,
        mesh=mesh,
        in_specs=(
            P("tm", "asset", None),
            P(),
            P(),
            P("tm", "asset", None),
            P("asset"),
            P("asset"),
            P("asset"),
            P("asset", None, None),
            P("asset"),
            P("asset"),
            P("asset"),
            P("asset", None, None),
        ),
        out_specs=(P("tm", "asset", None), P("tm", "asset", None), P(), P()),
        check_vma=False,
    )
```

```python
import functools

import jax
import jax.numpy as jnp
from jax import lax
from jax.experimental import pallas as pl
from jax.experimental.pallas import tpu as pltpu
from jax.sharding import PartitionSpec as P

MESH = pl.DeviceIdType.MESH
F32 = jnp.float32
BF16 = jnp.bfloat16
NX, NZ, NY, NC = 4, 4, 4, 2
STEPS, BLOCKS, TILE, D = 2, 10, 128, 512
PEERS = NX * NZ - 1
LOC = 20
ZERO = BLOCKS + LOC
ROWS = STEPS * BLOCKS
WIDE = 5
GROUP = 5
SCALE = float(16 * 20480) ** -0.5


HOPS = (1, 3, 2)
ORDER = [(s, 0) for s in HOPS] + [(0, j) for j in HOPS] + [(s, j) for s in HOPS for j in HOPS]


def pick(i, values):
    found = values[-1]
    for n, value in enumerate(values[:-1]):
        found = jnp.where(i == n, value, found)
    return found


def place():
    asset, tm = lax.axis_index("asset"), lax.axis_index("tm")
    return asset // NZ, asset % NZ, tm // NC, tm % NC


def at_distance(dx, dz):
    x, z, _, _ = place()
    return (x + dx) % NX * NZ + (z + dz) % NZ


def from_distance(dx, dz):
    return at_distance(NX - dx, NZ - dz)


def turned(h, first, second):
    return jnp.where(h == 0, first, second), jnp.where(h == 0, second, first)


def chain_tables(rows, cols, count, rrows, rcols, links, heads):
    live = count[0]

    def table(keys, way, start):
        for n, key in enumerate(keys):
            found = start(key)
            for m in range(n):
                found = jnp.where(keys[m] == key, BLOCKS + m, found)
            links[way, n] = found
        for r in range(BLOCKS):
            found = start(r)
            for m, key in enumerate(keys):
                found = jnp.where(key == r, BLOCKS + m, found)
            heads[way, r] = found

    for way, src in ((0, rows), (1, cols)):
        table([jnp.where(n < live, src[n], -1) for n in range(LOC)], way, lambda key: ZERO)
    for h in range(STEPS):
        for way, src in ((2, rrows), (4, rcols)):
            table([src[from_distance(*((s, j), (j, s))[h])] for s, j in ORDER], way + h, lambda key: key)


def dot(a, b, ca, cb):
    return lax.dot_general(a, b, (((ca,), (cb,)), ((), ())), preferred_element_type=F32)


def each(first, last, do):
    def step(k, _):
        do(k)
        return 0

    lax.fori_loop(first, last, step, 0)


def kernel(
    count, rows_hbm, cols_hbm, rrows_hbm, rcols_hbm, rlive_hbm,
    feat_hbm, cot_hbm, wv_hbm, wg_hbm, lt_hbm, rt_hbm,
    outs, gsum, gate, part, wv,
    rows, cols, rrows, rcols, rlive,
    feat, cot, wg, lt, rt,
    away, over, last, slots, dagg, dgate,
    full, core_in, acc, y_in, mine, mine_out, xz_in,
    links, heads,
    load_sem, ex_s, first_r, last_r,
    core_s, core_r, y_s, y_r, xz_s, xz_r,
):
    x, z, y, c = place()
    asset, tm = lax.axis_index("asset"), lax.axis_index("tm")

    loads = []
    for i, (src, dst) in enumerate(
        (
            (rcols_hbm, rcols),
            (rlive_hbm, rlive),
            (feat_hbm, feat),
            (rt_hbm, rt),
            (wg_hbm, wg),
            (cot_hbm, cot),
            (rows_hbm, rows),
            (cols_hbm, cols),
            (rrows_hbm, rrows),
            (lt_hbm, lt),
            (wv_hbm, wv),
        )
    ):
        copy = pltpu.make_async_copy(src, dst, load_sem.at[i])
        copy.start()
        loads.append(copy)

    def core_peer():
        return (y * NC + (1 - c), asset)

    def y_peer(dy):
        return ((y + dy) % NY * NC + c, asset)

    def other(k):
        return (asset + 1 + k) % (NX * NZ)

    barrier = pltpu.get_barrier_semaphore()
    each(0, PEERS, lambda k: pl.semaphore_signal(barrier, inc=1, device_id=(tm, other(k)), device_id_type=MESH))
    for dy in (1, 2, 3):
        pl.semaphore_signal(barrier, inc=1, device_id=y_peer(dy), device_id_type=MESH)
    pl.semaphore_signal(barrier, inc=1, device_id=core_peer(), device_id_type=MESH)

    def first_hop(e, h, d):
        return pltpu.make_async_remote_copy(
            src_ref=away.at[h, d - 1], dst_ref=over.at[e, h, d],
            send_sem=ex_s.at[e, 0], recv_sem=first_r.at[e, h, d - 1],
            device_id=(tm, at_distance(*turned(h, d, 0))), device_id_type=MESH,
        )

    def second_hop(e, h, s, j):
        return pltpu.make_async_remote_copy(
            src_ref=over.at[e, h, s, j], dst_ref=last.at[e, h, s, j - 1],
            send_sem=ex_s.at[e, 1], recv_sem=last_r.at[e, h, s],
            device_id=(tm, at_distance(*turned(h, 0, j))), device_id_type=MESH,
        )

    def masked(peer):
        return (rt[peer].astype(F32) * rlive[peer].astype(F32)).astype(BF16)

    def all_of(src, dst, ssem, rsem):
        return pltpu.make_async_remote_copy(
            src_ref=src, dst_ref=dst, send_sem=ssem, recv_sem=rsem, device_id=core_peer(), device_id_type=MESH
        )

    def arrived(e, h, s):
        all_of(last.at[e, h, s], last.at[e, h, s], ex_s.at[e, 1], last_r.at[e, h, s]).wait_recv()

    def send(e, block, ready):
        def fill(i):
            d, h = pick(i // 2, HOPS), i % 2
            for j in range(4):
                away[h, d - 1, j] = block(h, at_distance(*turned(h, d, j)))

        def go(i):
            first_hop(e, i % 2, pick(i // 2, HOPS)).start()

        def both(i):
            fill(i)
            go(i)

        fill(0)
        ready()
        go(0)
        each(1, 6, both)

        def own(h):
            for j in (1, 2, 3):
                over[e, h, 0, j] = block(h, at_distance(*turned(h, 0, j)))

        each(0, 2, own)

    def hand(e):
        def step(i):
            second_hop(e, i % 2, 0, pick(i // 2, HOPS)).start()

        each(0, 6, step)

    def relay(e, first, end):
        def step(i):
            s, h = pick(i // 2, HOPS), i % 2
            first_hop(e, h, s).wait_recv()
            for j in (1, 3, 2):
                second_hop(e, h, s, j).start()

        each(first, end, step)

    for copy in loads[:4]:
        copy.wait()

    def term(h, peer):
        return dot(masked(peer), feat[h * BLOCKS + rcols[peer]], 1, 0).astype(BF16)

    send(0, term, lambda: pl.semaphore_wait(barrier, PEERS + 4))
    hand(0)

    loads[4].wait()
    loads[5].wait()

    def gate_step(i):
        at = pl.ds(WIDE * i, WIDE)
        logits = dot(feat[at].reshape(WIDE * TILE, D), wg[...], 1, 0)
        g = jax.nn.sigmoid(logits).reshape(WIDE, TILE, D)
        gate[at] = g
        dagg[at] = (cot[at].astype(F32) * g).astype(BF16)

    each(0, ROWS // WIDE, gate_step)
    for copy in loads[6:10]:
        copy.wait()
    chain_tables(rows, cols, count, rrows, rcols, links, heads)
    slots[ZERO] = jnp.zeros((STEPS, TILE, D), F32)

    def local_chain(src, blocks, way, side):
        def entry(l):
            tile = lt[l]
            other_block = src[l]
            for t in range(STEPS):
                slots[BLOCKS + l, t] = slots[links[way, l], t] + dot(tile, blocks[t * BLOCKS + other_block], side, 0)

        each(0, LOC, entry)

        def base(r):
            slots[r] = slots[heads[way, r]]

        each(0, BLOCKS, base)

    local_chain(cols, feat, 0, 1)
    relay(0, 0, 6)

    def sent_away(e):
        all_of(away, away, ex_s.at[e, 0], first_r.at[e, 0, 0]).wait_send()

    sent_away(0)

    def owed(h, peer):
        return dagg[h * BLOCKS + rrows[peer]]

    send(1, owed, lambda: None)
    hand(1)

    def take_near(e, add):
        def direct(i):
            s, h = pick(i // 2, HOPS), i % 2
            add(i // 2, h, from_distance(*turned(h, s, 0)), over[e, h, s, 0])

        def handed(i):
            j, h = pick(i // 2, HOPS), i % 2
            add(3 + i // 2, h, from_distance(*turned(h, 0, j)), last[e, h, 0, j - 1])

        each(0, 6, direct)
        each(0, 2, lambda h: arrived(e, h, 0))
        each(0, 6, handed)

    def take_far(e, first, end, add):
        def across(i):
            n, h = i // 2, i % 2
            s = pick(n, HOPS)
            arrived(e, h, s)
            for m, j in enumerate(HOPS):
                add(6 + 3 * n + m, h, from_distance(*turned(h, s, j)), last[e, h, s, j - 1])

        each(first, end, across)

    def add_term(k, h, peer, block):
        slots[BLOCKS + k, h] = slots[links[2 + h, k], h] + block.astype(F32)

    take_near(0, add_term)
    take_far(0, 0, 6, add_term)
    loads[10].wait()

    def summed(way, i):
        t, r = WIDE * i // BLOCKS, WIDE * i % BLOCKS
        return jnp.concatenate([slots[heads[way + t, r + n], t] for n in range(WIDE)])

    def middle(i):
        at = pl.ds(WIDE * i, WIDE)
        total = summed(2, i)
        high = total.astype(BF16)
        low = (total - high.astype(F32)).astype(BF16)
        gsum[at] = high.reshape(WIDE, TILE, D)
        agg = (dot(high, wv[...], 1, 0) + dot(low, wv[...], 1, 0)).reshape(WIDE, TILE, D)
        g = gate[at]
        outs[at] = (feat[at].astype(F32) + g * agg).astype(BF16)
        dgate[at] = (cot[at].astype(F32) * agg * g * (1.0 - g)).astype(BF16)

    each(0, ROWS // WIDE, middle)
    def weight(n, left, right):
        def product(i):
            at = pl.ds(BLOCKS * i, BLOCKS)
            return dot(left[at].reshape(BLOCKS * TILE, D), right[at].reshape(BLOCKS * TILE, D), 0, 0)

        part[n] = product(0)
        part[n] += product(1)

    core_copy = pltpu.make_async_remote_copy(
        src_ref=part.at[1 - c], dst_ref=core_in, send_sem=core_s.at[0], recv_sem=core_r.at[0],
        device_id=core_peer(), device_id_type=MESH,
    )
    weight(0, gsum, dagg)

    @pl.when(c == 1)
    def _():
        core_copy.start()

    weight(1, feat, dgate)

    @pl.when(c == 0)
    def _():
        core_copy.start()

    core_copy.wait_recv()
    acc[...] = (part[c] + core_in[...]).astype(BF16)

    def y_copy(dy):
        return pltpu.make_async_remote_copy(
            src_ref=acc.at[pl.ds((y + dy) % NY * TILE, TILE)], dst_ref=y_in.at[dy - 1],
            send_sem=y_s.at[0], recv_sem=y_r.at[0], device_id=y_peer(dy), device_id_type=MESH,
        )

    y_copies = [y_copy(dy) for dy in (1, 3, 2)]
    for copy in y_copies:
        copy.start()

    local_chain(rows, dagg, 1, 0)
    own_rows = pl.ds(y * TILE, TILE)
    mine[...] = part[c, own_rows, :] + core_in[own_rows, :]

    y_all = all_of(y_in, y_in, y_s.at[0], y_r.at[0])
    y_all.wait_recv()
    mine[...] += y_in[0].astype(F32) + y_in[1].astype(F32) + y_in[2].astype(F32)
    mine_out[...] = mine[...].reshape(NX * NZ, 8, D).astype(BF16)

    def spread(k):
        return pltpu.make_async_remote_copy(
            src_ref=mine_out.at[other(k)], dst_ref=xz_in.at[k],
            send_sem=xz_s.at[0], recv_sem=xz_r.at[0], device_id=(tm, other(k)), device_id_type=MESH,
        )

    def gather(k):
        return pltpu.make_async_remote_copy(
            src_ref=full.at[c, y, asset], dst_ref=full.at[c, y, asset],
            send_sem=xz_s.at[1], recv_sem=xz_r.at[1 + k // GROUP], device_id=(tm, other(k)), device_id_type=MESH,
        )

    each(0, PEERS, lambda k: spread(k).start())
    relay(1, 0, 2)

    def pre_step(i):
        at = pl.ds(WIDE * i, WIDE)
        gate[at] = cot[at].astype(F32) + dot(dgate[at].reshape(WIDE * TILE, D), wg[...], 1, 1).reshape(WIDE, TILE, D)

    each(0, ROWS // WIDE, pre_step)

    spread_all = all_of(xz_in, xz_in, xz_s.at[0], xz_r.at[0])
    spread_all.wait_recv()
    total = mine[pl.ds(asset * 8, 8), :]
    for k in range(PEERS):
        total = total + xz_in[k].astype(F32)
    full[c, y, asset] = (total * SCALE).astype(BF16)
    each(0, PEERS, lambda k: gather(k).start())

    def add_back(k, h, peer, block):
        slots[BLOCKS + k, h] = slots[links[4 + h, k], h] + dot(masked(peer), block, 0, 0)

    relay(1, 2, 6)
    take_near(1, add_back)

    def hand_y(k, dy):
        piece = full.at[c, y, (asset + NX * NZ - 1 - k) % (NX * NZ)]
        return pltpu.make_async_remote_copy(
            src_ref=piece, dst_ref=piece, send_sem=y_s.at[1], recv_sem=y_r.at[1],
            device_id=y_peer(dy), device_id_type=MESH,
        )

    some = full.at[c, y, pl.ds(0, GROUP)]

    def pass_on(g):
        all_of(some, some, xz_s.at[1], xz_r.at[1 + g]).wait_recv()
        for k in range(GROUP):
            for dy in (1, 3, 2):
                hand_y(g * GROUP + k, dy).start()

    for dy in (1, 3, 2):
        hand_y(PEERS, dy).start()
    each(0, PEERS // GROUP, pass_on)
    take_far(1, 0, 4, add_back)
    most = full.at[c, pl.ds(0, NY - 1)]
    hand_all = all_of(most, most, y_s.at[1], y_r.at[1])
    hand_all.wait_recv()
    core_gather = pltpu.make_async_remote_copy(
        src_ref=full.at[c], dst_ref=full.at[c], send_sem=core_s.at[1], recv_sem=core_r.at[1],
        device_id=core_peer(), device_id_type=MESH,
    )
    core_gather.start()
    core_copy.wait_send()
    core_gather.wait_recv()
    for n in range(2):
        part[n] = full[n].astype(F32).reshape(D, D)
    take_far(1, 4, 6, add_back)

    def settle(i):
        gsum[pl.ds(WIDE * i, WIDE)] = summed(4, i).astype(BF16).reshape(WIDE, TILE, D)

    each(0, ROWS // WIDE, settle)
    sent_away(1)
    for e in range(2):
        all_of(last.at[e], last.at[e], ex_s.at[e, 1], last_r.at[e, 0, 0]).wait_send()
    y_all.wait_send()
    spread_all.wait_send()
    pieces = full.at[c, y, pl.ds(0, PEERS)]
    all_of(pieces, pieces, xz_s.at[1], xz_r.at[1]).wait_send()
    hand_all.wait_send()
    core_gather.wait_send()


def emit(outs, dvalue, rest, part, wv, out_hbm, gf_hbm, gv_hbm, gg_hbm, grads, sem):
    copies = [pltpu.make_async_copy(outs, out_hbm, sem.at[0])]
    copies[0].start()
    for i, dst in enumerate((gv_hbm, gg_hbm)):
        copies.append(pltpu.make_async_copy(part.at[i], dst, sem.at[1 + i]))
        copies[-1].start()

    def chunk(i):
        at = pl.ds(WIDE * i, WIDE)
        return at, pltpu.make_async_copy(grads.at[at], gf_hbm.at[at], sem.at[3 + i])

    def finish(i):
        at, copy = chunk(i)
        back = dot(dvalue[at].reshape(WIDE * TILE, D), wv[...], 1, 1).reshape(WIDE, TILE, D)
        grads[at] = (rest[at] + back).astype(BF16)
        copy.start()

    each(0, ROWS // WIDE, finish)
    each(0, ROWS // WIDE, lambda i: chunk(i)[1].wait())
    for copy in copies:
        copy.wait()


def per_device(
    features, w_value, w_gate, cotangent, local_rows, local_cols, local_count, local_tiles,
    remote_rows, remote_cols, remote_live, remote_tiles,
):
    hbm = pl.BlockSpec(memory_space=pl.ANY)
    vmem = pl.BlockSpec(memory_space=pltpu.VMEM)
    dma = pltpu.SemaphoreType.DMA
    blocks = (ROWS, TILE, D)
    tables = (local_rows, local_cols, remote_rows, remote_cols, remote_live)
    reduced = (2, NY, NX * NZ, 8, D)
    held = pl.pallas_call(
        kernel,
        name="relation",
        out_shape=(
            pltpu.VMEM(blocks, BF16),
            pltpu.VMEM(blocks, BF16),
            pltpu.VMEM(blocks, F32),
            pltpu.VMEM((2, D, D), F32),
            pltpu.VMEM((D, D), BF16),
        ),
        in_specs=[pl.BlockSpec(memory_space=pltpu.SMEM)] + [hbm] * 11,
        out_specs=(vmem,) * 5,
        scratch_shapes=[
            *(pltpu.SMEM(a.shape, jnp.int32) for a in tables),
            pltpu.VMEM(blocks, BF16),
            pltpu.VMEM(blocks, BF16),
            pltpu.VMEM((D, D), BF16),
            pltpu.VMEM((LOC, TILE, TILE), BF16),
            pltpu.VMEM((NX * NZ, TILE, TILE), BF16),
            pltpu.VMEM((2, 3, 4, TILE, D), BF16),
            pltpu.VMEM((2, 2, 4, 4, TILE, D), BF16),
            pltpu.VMEM((2, 2, 4, 3, TILE, D), BF16),
            pltpu.VMEM((ZERO + 1, STEPS, TILE, D), F32),
            pltpu.VMEM(blocks, BF16),
            pltpu.VMEM(blocks, BF16),
            pltpu.VMEM(reduced, BF16),
            pltpu.VMEM((D, D), F32),
            pltpu.VMEM((D, D), BF16),
            pltpu.VMEM((NY - 1, TILE, D), BF16),
            pltpu.VMEM((TILE, D), F32),
            pltpu.VMEM((NX * NZ, 8, D), BF16),
            pltpu.VMEM((PEERS, 8, D), BF16),
            pltpu.SMEM((6, LOC), jnp.int32),
            pltpu.SMEM((6, BLOCKS), jnp.int32),
            dma((11,)),
            dma((2, 2)),
            dma((2, 2, 3)),
            dma((2, 2, 4)),
            dma((2,)),
            dma((2,)),
            dma((2,)),
            dma((2,)),
            dma((2,)),
            dma((1 + PEERS // GROUP,)),
        ],
        compiler_params=pltpu.CompilerParams(
            collective_id=0, has_side_effects=True, vmem_limit_bytes=53000000
        ),
    )(
        local_count, *tables,
        features.reshape(blocks), cotangent.reshape(blocks), w_value, w_gate, local_tiles, remote_tiles,
    )
    square = jax.ShapeDtypeStruct((D, D), F32)
    out, grad, gv, gg = pl.pallas_call(
        emit,
        name="emit",
        out_shape=(jax.ShapeDtypeStruct(blocks, BF16), jax.ShapeDtypeStruct(blocks, BF16), square, square),
        in_specs=[vmem] * 5,
        out_specs=(hbm,) * 4,
        scratch_shapes=[pltpu.VMEM(blocks, BF16), dma((3 + ROWS // WIDE,))],
        compiler_params=pltpu.CompilerParams(vmem_limit_bytes=16 << 20),
    )(*[pltpu.with_memory_space_constraint(a, pltpu.MemorySpace.VMEM) for a in held])
    return (
        out.reshape(features.shape),
        grad.reshape(features.shape),
        gv,
        gg,
    )


def solution(mesh):
    return jax.shard_map(
        per_device,
        mesh=mesh,
        in_specs=(
            P("tm", "asset", None),
            P(),
            P(),
            P("tm", "asset", None),
            P("asset"),
            P("asset"),
            P("asset"),
            P("asset", None, None),
            P("asset"),
            P("asset"),
            P("asset"),
            P("asset", None, None),
        ),
        out_specs=(P("tm", "asset", None), P("tm", "asset", None), P(), P()),
        check_vma=False,
    )
```

```python
import functools

import jax
import jax.numpy as jnp
from jax import lax
from jax.experimental import pallas as pl
from jax.experimental.pallas import tpu as pltpu
from jax.sharding import PartitionSpec as P

MESH = pl.DeviceIdType.MESH
F32 = jnp.float32
BF16 = jnp.bfloat16
NX, NZ, NY, NC = 4, 4, 4, 2
STEPS, BLOCKS, TILE, D = 2, 10, 128, 512
PEERS = NX * NZ - 1
LOC = 20
ZERO = BLOCKS + LOC
ROWS = STEPS * BLOCKS
WIDE = 5
GROUP = 5
SCALE = float(16 * 20480) ** -0.5


HOPS = (1, 3, 2)
ORDER = [(s, 0) for s in HOPS] + [(0, j) for j in HOPS] + [(s, j) for s in HOPS for j in HOPS]


def pick(i, values):
    found = values[-1]
    for n, value in enumerate(values[:-1]):
        found = jnp.where(i == n, value, found)
    return found


def place():
    asset, tm = lax.axis_index("asset"), lax.axis_index("tm")
    return asset // NZ, asset % NZ, tm // NC, tm % NC


def at_distance(dx, dz):
    x, z, _, _ = place()
    return (x + dx) % NX * NZ + (z + dz) % NZ


def from_distance(dx, dz):
    return at_distance(NX - dx, NZ - dz)


def turned(h, first, second):
    return jnp.where(h == 0, first, second), jnp.where(h == 0, second, first)


def chain_tables(rows, cols, count, rrows, rcols, links, heads):
    live = count[0]

    def table(keys, way, start):
        for n, key in enumerate(keys):
            found = start(key)
            for m in range(n):
                found = jnp.where(keys[m] == key, BLOCKS + m, found)
            links[way, n] = found
        for r in range(BLOCKS):
            found = start(r)
            for m, key in enumerate(keys):
                found = jnp.where(key == r, BLOCKS + m, found)
            heads[way, r] = found

    for way, src in ((0, rows), (1, cols)):
        table([jnp.where(n < live, src[n], -1) for n in range(LOC)], way, lambda key: ZERO)
    for h in range(STEPS):
        for way, src in ((2, rrows), (4, rcols)):
            table([src[from_distance(*((s, j), (j, s))[h])] for s, j in ORDER], way + h, lambda key: key)


def dot(a, b, ca, cb):
    return lax.dot_general(a, b, (((ca,), (cb,)), ((), ())), preferred_element_type=F32)


def each(first, last, do):
    def step(k, _):
        do(k)
        return 0

    lax.fori_loop(first, last, step, 0)


def kernel(
    count, rows_hbm, cols_hbm, rrows_hbm, rcols_hbm, rlive_hbm,
    feat_hbm, cot_hbm, wv_hbm, wg_hbm, lt_hbm, rt_hbm,
    outs, gsum, gate, part, wv,
    rows, cols, rrows, rcols, rlive,
    feat, cot, wg, lt, rt,
    away, over, last, slots, dagg, dgate,
    full, core_in, acc, y_in, mine, mine_out, xz_in,
    links, heads,
    load_sem, ex_s, first_r, last_r,
    core_s, core_r, y_s, y_r, xz_s, xz_r,
):
    x, z, y, c = place()
    asset, tm = lax.axis_index("asset"), lax.axis_index("tm")

    loads = []
    for i, (src, dst) in enumerate(
        (
            (rcols_hbm, rcols),
            (rlive_hbm, rlive),
            (feat_hbm, feat),
            (rt_hbm, rt),
            (wg_hbm, wg),
            (cot_hbm, cot),
            (rows_hbm, rows),
            (cols_hbm, cols),
            (rrows_hbm, rrows),
            (lt_hbm, lt),
            (wv_hbm, wv),
        )
    ):
        loads.append(pltpu.make_async_copy(src, dst, load_sem.at[i]))
    for copy in loads[:4]:
        copy.start()

    def core_peer():
        return (y * NC + (1 - c), asset)

    def y_peer(dy):
        return ((y + dy) % NY * NC + c, asset)

    def other(k):
        return (asset + 1 + k) % (NX * NZ)

    barrier = pltpu.get_barrier_semaphore()
    each(0, PEERS, lambda k: pl.semaphore_signal(barrier, inc=1, device_id=(tm, other(k)), device_id_type=MESH))
    for dy in (1, 2, 3):
        pl.semaphore_signal(barrier, inc=1, device_id=y_peer(dy), device_id_type=MESH)
    pl.semaphore_signal(barrier, inc=1, device_id=core_peer(), device_id_type=MESH)

    def first_hop(e, h, d):
        return pltpu.make_async_remote_copy(
            src_ref=away.at[h, d - 1], dst_ref=over.at[e, h, d],
            send_sem=ex_s.at[e, 0], recv_sem=first_r.at[e, h, d - 1],
            device_id=(tm, at_distance(*turned(h, d, 0))), device_id_type=MESH,
        )

    def second_hop(e, h, s, j):
        return pltpu.make_async_remote_copy(
            src_ref=over.at[e, h, s, j], dst_ref=last.at[e, h, s, j - 1],
            send_sem=ex_s.at[e, 1], recv_sem=last_r.at[e, h, s],
            device_id=(tm, at_distance(*turned(h, 0, j))), device_id_type=MESH,
        )

    def masked(peer):
        return (rt[peer].astype(F32) * rlive[peer].astype(F32)).astype(BF16)

    def all_of(src, dst, ssem, rsem):
        return pltpu.make_async_remote_copy(
            src_ref=src, dst_ref=dst, send_sem=ssem, recv_sem=rsem, device_id=core_peer(), device_id_type=MESH
        )

    def arrived(e, h, s):
        all_of(last.at[e, h, s], last.at[e, h, s], ex_s.at[e, 1], last_r.at[e, h, s]).wait_recv()

    def send(e, block, ready):
        def fill(i):
            d, h = pick(i // 2, HOPS), i % 2
            for j in range(4):
                away[h, d - 1, j] = block(h, at_distance(*turned(h, d, j)))

        def go(i):
            first_hop(e, i % 2, pick(i // 2, HOPS)).start()

        def both(i):
            fill(i)
            go(i)

        fill(0)
        ready()
        go(0)
        each(1, 6, both)

        def own(h):
            for j in (1, 2, 3):
                over[e, h, 0, j] = block(h, at_distance(*turned(h, 0, j)))

        each(0, 2, own)

    def hand(e):
        def step(i):
            second_hop(e, i % 2, 0, pick(i // 2, HOPS)).start()

        each(0, 6, step)

    def relay(e, first, end):
        def step(i):
            s, h = pick(i // 2, HOPS), i % 2
            first_hop(e, h, s).wait_recv()
            for j in (1, 3, 2):
                second_hop(e, h, s, j).start()

        each(first, end, step)

    for copy in loads[:4]:
        copy.wait()
    for copy in loads[4:]:
        copy.start()

    def term(h, peer):
        return dot(masked(peer), feat[h * BLOCKS + rcols[peer]], 1, 0).astype(BF16)

    send(0, term, lambda: pl.semaphore_wait(barrier, PEERS + 4))
    hand(0)

    loads[4].wait()
    loads[5].wait()

    def gate_step(i):
        at = pl.ds(WIDE * i, WIDE)
        logits = dot(feat[at].reshape(WIDE * TILE, D), wg[...], 1, 0)
        g = jax.nn.sigmoid(logits).reshape(WIDE, TILE, D)
        gate[at] = g
        dagg[at] = (cot[at].astype(F32) * g).astype(BF16)

    each(0, ROWS // WIDE, gate_step)
    for copy in loads[6:10]:
        copy.wait()
    chain_tables(rows, cols, count, rrows, rcols, links, heads)
    slots[ZERO] = jnp.zeros((STEPS, TILE, D), F32)

    def local_chain(src, blocks, way, side):
        def entry(l):
            tile = lt[l]
            other_block = src[l]
            for t in range(STEPS):
                slots[BLOCKS + l, t] = slots[links[way, l], t] + dot(tile, blocks[t * BLOCKS + other_block], side, 0)

        each(0, LOC, entry)

        def base(r):
            slots[r] = slots[heads[way, r]]

        each(0, BLOCKS, base)

    local_chain(cols, feat, 0, 1)
    relay(0, 0, 6)

    def sent_away(e):
        all_of(away, away, ex_s.at[e, 0], first_r.at[e, 0, 0]).wait_send()

    sent_away(0)

    def owed(h, peer):
        return dagg[h * BLOCKS + rrows[peer]]

    send(1, owed, lambda: None)
    hand(1)

    def take_near(e, add):
        def direct(i):
            s, h = pick(i // 2, HOPS), i % 2
            add(i // 2, h, from_distance(*turned(h, s, 0)), over[e, h, s, 0])

        def handed(i):
            j, h = pick(i // 2, HOPS), i % 2
            add(3 + i // 2, h, from_distance(*turned(h, 0, j)), last[e, h, 0, j - 1])

        each(0, 6, direct)
        each(0, 2, lambda h: arrived(e, h, 0))
        each(0, 6, handed)

    def take_far(e, first, end, add):
        def across(i):
            n, h = i // 2, i % 2
            s = pick(n, HOPS)
            arrived(e, h, s)
            for m, j in enumerate(HOPS):
                add(6 + 3 * n + m, h, from_distance(*turned(h, s, j)), last[e, h, s, j - 1])

        each(first, end, across)

    def add_term(k, h, peer, block):
        slots[BLOCKS + k, h] = slots[links[2 + h, k], h] + block.astype(F32)

    take_near(0, add_term)
    take_far(0, 0, 6, add_term)
    loads[10].wait()

    def summed(way, i):
        t, r = WIDE * i // BLOCKS, WIDE * i % BLOCKS
        return jnp.concatenate([slots[heads[way + t, r + n], t] for n in range(WIDE)])

    def middle(i):
        at = pl.ds(WIDE * i, WIDE)
        total = summed(2, i)
        high = total.astype(BF16)
        low = (total - high.astype(F32)).astype(BF16)
        gsum[at] = high.reshape(WIDE, TILE, D)
        agg = (dot(high, wv[...], 1, 0) + dot(low, wv[...], 1, 0)).reshape(WIDE, TILE, D)
        g = gate[at]
        outs[at] = (feat[at].astype(F32) + g * agg).astype(BF16)
        dgate[at] = (cot[at].astype(F32) * agg * g * (1.0 - g)).astype(BF16)

    each(0, ROWS // WIDE, middle)
    def weight(n, left, right):
        def product(i):
            at = pl.ds(BLOCKS * i, BLOCKS)
            return dot(left[at].reshape(BLOCKS * TILE, D), right[at].reshape(BLOCKS * TILE, D), 0, 0)

        part[n] = product(0)
        part[n] += product(1)

    core_copy = pltpu.make_async_remote_copy(
        src_ref=part.at[1 - c], dst_ref=core_in, send_sem=core_s.at[0], recv_sem=core_r.at[0],
        device_id=core_peer(), device_id_type=MESH,
    )
    weight(0, gsum, dagg)

    @pl.when(c == 1)
    def _():
        core_copy.start()

    weight(1, feat, dgate)

    @pl.when(c == 0)
    def _():
        core_copy.start()

    core_copy.wait_recv()
    acc[...] = (part[c] + core_in[...]).astype(BF16)

    def y_copy(dy):
        return pltpu.make_async_remote_copy(
            src_ref=acc.at[pl.ds((y + dy) % NY * TILE, TILE)], dst_ref=y_in.at[dy - 1],
            send_sem=y_s.at[0], recv_sem=y_r.at[0], device_id=y_peer(dy), device_id_type=MESH,
        )

    y_copies = [y_copy(dy) for dy in (1, 3, 2)]
    for copy in y_copies:
        copy.start()

    local_chain(rows, dagg, 1, 0)
    own_rows = pl.ds(y * TILE, TILE)
    mine[...] = part[c, own_rows, :] + core_in[own_rows, :]

    y_all = all_of(y_in, y_in, y_s.at[0], y_r.at[0])
    y_all.wait_recv()
    mine[...] += y_in[0].astype(F32) + y_in[1].astype(F32) + y_in[2].astype(F32)
    mine_out[...] = mine[...].reshape(NX * NZ, 8, D).astype(BF16)

    def spread(k):
        return pltpu.make_async_remote_copy(
            src_ref=mine_out.at[other(k)], dst_ref=xz_in.at[k],
            send_sem=xz_s.at[0], recv_sem=xz_r.at[0], device_id=(tm, other(k)), device_id_type=MESH,
        )

    def gather(k):
        return pltpu.make_async_remote_copy(
            src_ref=full.at[c, y, asset], dst_ref=full.at[c, y, asset],
            send_sem=xz_s.at[1], recv_sem=xz_r.at[1 + k // GROUP], device_id=(tm, other(k)), device_id_type=MESH,
        )

    each(0, PEERS, lambda k: spread(k).start())
    relay(1, 0, 2)

    def pre_step(i):
        at = pl.ds(WIDE * i, WIDE)
        gate[at] = cot[at].astype(F32) + dot(dgate[at].reshape(WIDE * TILE, D), wg[...], 1, 1).reshape(WIDE, TILE, D)

    each(0, ROWS // WIDE, pre_step)

    spread_all = all_of(xz_in, xz_in, xz_s.at[0], xz_r.at[0])
    spread_all.wait_recv()
    total = mine[pl.ds(asset * 8, 8), :]
    for k in range(PEERS):
        total = total + xz_in[k].astype(F32)
    full[c, y, asset] = (total * SCALE).astype(BF16)
    each(0, PEERS, lambda k: gather(k).start())

    def add_back(k, h, peer, block):
        slots[BLOCKS + k, h] = slots[links[4 + h, k], h] + dot(masked(peer), block, 0, 0)

    relay(1, 2, 6)
    take_near(1, add_back)

    def hand_y(k, dy):
        piece = full.at[c, y, (asset + NX * NZ - 1 - k) % (NX * NZ)]
        return pltpu.make_async_remote_copy(
            src_ref=piece, dst_ref=piece, send_sem=y_s.at[1], recv_sem=y_r.at[1],
            device_id=y_peer(dy), device_id_type=MESH,
        )

    some = full.at[c, y, pl.ds(0, GROUP)]

    def pass_on(g):
        all_of(some, some, xz_s.at[1], xz_r.at[1 + g]).wait_recv()
        for k in range(GROUP):
            for dy in (1, 3, 2):
                hand_y(g * GROUP + k, dy).start()

    for dy in (1, 3, 2):
        hand_y(PEERS, dy).start()
    each(0, PEERS // GROUP, pass_on)
    take_far(1, 0, 4, add_back)
    most = full.at[c, pl.ds(0, NY - 1)]
    hand_all = all_of(most, most, y_s.at[1], y_r.at[1])
    hand_all.wait_recv()
    core_gather = pltpu.make_async_remote_copy(
        src_ref=full.at[c], dst_ref=full.at[c], send_sem=core_s.at[1], recv_sem=core_r.at[1],
        device_id=core_peer(), device_id_type=MESH,
    )
    core_gather.start()
    core_copy.wait_send()
    core_gather.wait_recv()
    for n in range(2):
        part[n] = full[n].astype(F32).reshape(D, D)
    take_far(1, 4, 6, add_back)

    def settle(i):
        gsum[pl.ds(WIDE * i, WIDE)] = summed(4, i).astype(BF16).reshape(WIDE, TILE, D)

    each(0, ROWS // WIDE, settle)
    sent_away(1)
    for e in range(2):
        all_of(last.at[e], last.at[e], ex_s.at[e, 1], last_r.at[e, 0, 0]).wait_send()
    y_all.wait_send()
    spread_all.wait_send()
    pieces = full.at[c, y, pl.ds(0, PEERS)]
    all_of(pieces, pieces, xz_s.at[1], xz_r.at[1]).wait_send()
    hand_all.wait_send()
    core_gather.wait_send()


def emit(outs, dvalue, rest, part, wv, out_hbm, gf_hbm, gv_hbm, gg_hbm, grads, sem):
    copies = [pltpu.make_async_copy(outs, out_hbm, sem.at[0])]
    copies[0].start()
    for i, dst in enumerate((gv_hbm, gg_hbm)):
        copies.append(pltpu.make_async_copy(part.at[i], dst, sem.at[1 + i]))
        copies[-1].start()

    def chunk(i):
        at = pl.ds(WIDE * i, WIDE)
        return at, pltpu.make_async_copy(grads.at[at], gf_hbm.at[at], sem.at[3 + i])

    def finish(i):
        at, copy = chunk(i)
        back = dot(dvalue[at].reshape(WIDE * TILE, D), wv[...], 1, 1).reshape(WIDE, TILE, D)
        grads[at] = (rest[at] + back).astype(BF16)
        copy.start()

    each(0, ROWS // WIDE, finish)
    each(0, ROWS // WIDE, lambda i: chunk(i)[1].wait())
    for copy in copies:
        copy.wait()


def per_device(
    features, w_value, w_gate, cotangent, local_rows, local_cols, local_count, local_tiles,
    remote_rows, remote_cols, remote_live, remote_tiles,
):
    hbm = pl.BlockSpec(memory_space=pl.ANY)
    vmem = pl.BlockSpec(memory_space=pltpu.VMEM)
    dma = pltpu.SemaphoreType.DMA
    blocks = (ROWS, TILE, D)
    tables = (local_rows, local_cols, remote_rows, remote_cols, remote_live)
    reduced = (2, NY, NX * NZ, 8, D)
    held = pl.pallas_call(
        kernel,
        name="relation",
        out_shape=(
            pltpu.VMEM(blocks, BF16),
            pltpu.VMEM(blocks, BF16),
            pltpu.VMEM(blocks, F32),
            pltpu.VMEM((2, D, D), F32),
            pltpu.VMEM((D, D), BF16),
        ),
        in_specs=[pl.BlockSpec(memory_space=pltpu.SMEM)] + [hbm] * 11,
        out_specs=(vmem,) * 5,
        scratch_shapes=[
            *(pltpu.SMEM(a.shape, jnp.int32) for a in tables),
            pltpu.VMEM(blocks, BF16),
            pltpu.VMEM(blocks, BF16),
            pltpu.VMEM((D, D), BF16),
            pltpu.VMEM((LOC, TILE, TILE), BF16),
            pltpu.VMEM((NX * NZ, TILE, TILE), BF16),
            pltpu.VMEM((2, 3, 4, TILE, D), BF16),
            pltpu.VMEM((2, 2, 4, 4, TILE, D), BF16),
            pltpu.VMEM((2, 2, 4, 3, TILE, D), BF16),
            pltpu.VMEM((ZERO + 1, STEPS, TILE, D), F32),
            pltpu.VMEM(blocks, BF16),
            pltpu.VMEM(blocks, BF16),
            pltpu.VMEM(reduced, BF16),
            pltpu.VMEM((D, D), F32),
            pltpu.VMEM((D, D), BF16),
            pltpu.VMEM((NY - 1, TILE, D), BF16),
            pltpu.VMEM((TILE, D), F32),
            pltpu.VMEM((NX * NZ, 8, D), BF16),
            pltpu.VMEM((PEERS, 8, D), BF16),
            pltpu.SMEM((6, LOC), jnp.int32),
            pltpu.SMEM((6, BLOCKS), jnp.int32),
            dma((11,)),
            dma((2, 2)),
            dma((2, 2, 3)),
            dma((2, 2, 4)),
            dma((2,)),
            dma((2,)),
            dma((2,)),
            dma((2,)),
            dma((2,)),
            dma((1 + PEERS // GROUP,)),
        ],
        compiler_params=pltpu.CompilerParams(
            collective_id=0, has_side_effects=True, vmem_limit_bytes=53000000
        ),
    )(
        local_count, *tables,
        features.reshape(blocks), cotangent.reshape(blocks), w_value, w_gate, local_tiles, remote_tiles,
    )
    square = jax.ShapeDtypeStruct((D, D), F32)
    out, grad, gv, gg = pl.pallas_call(
        emit,
        name="emit",
        out_shape=(jax.ShapeDtypeStruct(blocks, BF16), jax.ShapeDtypeStruct(blocks, BF16), square, square),
        in_specs=[vmem] * 5,
        out_specs=(hbm,) * 4,
        scratch_shapes=[pltpu.VMEM(blocks, BF16), dma((3 + ROWS // WIDE,))],
        compiler_params=pltpu.CompilerParams(vmem_limit_bytes=16 << 20),
    )(*[pltpu.with_memory_space_constraint(a, pltpu.MemorySpace.VMEM) for a in held])
    return (
        out.reshape(features.shape),
        grad.reshape(features.shape),
        gv,
        gg,
    )


def solution(mesh):
    return jax.shard_map(
        per_device,
        mesh=mesh,
        in_specs=(
            P("tm", "asset", None),
            P(),
            P(),
            P("tm", "asset", None),
            P("asset"),
            P("asset"),
            P("asset"),
            P("asset", None, None),
            P("asset"),
            P("asset"),
            P("asset"),
            P("asset", None, None),
        ),
        out_specs=(P("tm", "asset", None), P("tm", "asset", None), P(), P()),
        check_vma=False,
    )
```
